32 devices in a mesh: wide: 8 (over y, x, core), narrow: 4 (over z).
Axes of the slice: x: 2, y: 2, z: 4, core: 2. Of those that a mesh axis runs over, the one named last changes fastest.
Arguments:
- features: bfloat16 [131072, 512], P(('wide', 'narrow')), may hold values from -6 to 6
- adjacency: bfloat16 [3072, 128, 128], P(('wide', 'narrow')), may hold values from -0.375 to 0.375
- block_rows: int32 [32, 96], P(('wide', 'narrow')), may hold values from 0 to 31, as said below
- block_cols: int32 [32, 96], P(('wide', 'narrow')), may hold values from 0 to 39, as said below
- block_count: int32 [32], P(('wide', 'narrow')), may hold values from 40 to 96, as said below
- node_count: int32 [32], P(('wide', 'narrow')), may hold values from 2048 to 4096, as said below
- halo_index: int32 [32, 4, 256], P(('wide', 'narrow')), may hold values from 0 to 2047, as said below
- weight: bfloat16 [512, 512], replicated, may hold values from -0.25 to 0.25
- bias: float32 [512], replicated, may hold values from -3 to 3
- out_grad: bfloat16 [131072, 512], P(('wide', 'narrow')), may hold values from -6 to 6
Outputs:
- output: bfloat16 [131072, 512], P(('wide', 'narrow'))
- input_grad: bfloat16 [131072, 512], P(('wide', 'narrow'))
- weight_grad: float32 [512, 512], replicated
- bias_grad: float32 [512], replicated
The draws below stay inside these ranges and needn't reach their ends.
Inputs may be any that keep to these rules, and one draw needn't show every extreme that they name: `block_count`: each device's live slots include every one of its 32 diagonal blocks and every one of its 8 halo column blocks at least once; some device has all 96 slots live. `block_rows`: within range for live and non-live slots. `block_cols`: within range for live and non-live slots. `node_count`: some device has all 4096 slots live. `halo_index`: the 1024 rows of one device are distinct and all live.
All inputs are finite; a program needn't handle non-finite values.
Results may differ from the reference program's by a relative error of at most 0.0062.
Values may be sent and summed in bfloat16 or wider, within the bound.
A program may use at most 192 MiB of HBM per device.

```python
import math
import jax
import jax.numpy as jnp
from jax import lax

F = 512
BS = 128
NODE_DEV = 4096
HALO = 256
RB = 32
ECB = 40
BLK = 96
TOTAL = 131072
N_WIDE = 8
N_NARROW = 4
DEVICES = 32


def layout_tables(key):
    key_count = jax.random.fold_in(key, 11)
    key_hot = jax.random.fold_in(key, 12)
    key_cold = jax.random.fold_in(key, 13)
    key_rows = jax.random.fold_in(key, 14)
    key_extra = jax.random.fold_in(key, 15)
    key_perm = jax.random.fold_in(key, 16)
    spare = BLK - ECB
    draws = jax.random.randint(key_count, (DEVICES,), 0, spare + 1)
    count = ECB + draws * draws // max(spare, 1)
    hot = jax.random.randint(key_hot, (), 0, DEVICES)
    cold = (hot + 1 + jax.random.randint(key_cold, (), 0, DEVICES - 1)) % DEVICES
    count = count.at[hot].set(BLK).at[cold].set(ECB)
    halo_rowsel = jax.random.randint(key_rows, (DEVICES, ECB - RB), 0, RB)
    fixed_rows = jnp.concatenate([jnp.broadcast_to(jnp.arange(RB, dtype=jnp.int32), (DEVICES, RB)), halo_rowsel.astype(jnp.int32)], 1)
    fixed_cols = jnp.broadcast_to(jnp.arange(ECB, dtype=jnp.int32), (DEVICES, ECB))
    perm_keys = jax.random.split(key_perm, DEVICES)
    perms = jax.vmap(lambda k: jax.random.permutation(k, ECB))(perm_keys)
    fixed_rows = jnp.take_along_axis(fixed_rows, perms, 1)
    fixed_cols = jnp.take_along_axis(fixed_cols, perms, 1)
    extra_rows = jax.random.randint(jax.random.fold_in(key_extra, 1), (DEVICES, spare), 0, RB)
    extra_cols = jax.random.randint(jax.random.fold_in(key_extra, 2), (DEVICES, spare), 0, ECB)
    rows = jnp.concatenate([fixed_rows, extra_rows.astype(jnp.int32)], 1)
    cols = jnp.concatenate([fixed_cols, extra_cols.astype(jnp.int32)], 1)
    return (rows, cols, count.astype(jnp.int32))


def draw_block_rows(key, part):
    return layout_tables(key)[0]


def draw_block_cols(key, part):
    return layout_tables(key)[1]


def draw_block_count(key, part):
    return layout_tables(key)[2]


def draw_node_count(key, part):
    counts = jax.random.randint(jax.random.fold_in(key, 21), (DEVICES,), NODE_DEV // 2, NODE_DEV + 1)
    full = jax.random.randint(jax.random.fold_in(key, 22), (), 0, DEVICES)
    return counts.at[full].set(NODE_DEV).astype(jnp.int32)


def draw_halo_index(key, part):
    keys = jax.random.split(jax.random.fold_in(key, 31), DEVICES)
    picks = jax.vmap(lambda k: jax.random.permutation(k, NODE_DEV // 2)[:4 * HALO])(keys)
    return picks.reshape(DEVICES, 4, HALO).astype(jnp.int32)


def levels(own_key, shape, shards, low, largest):
    def one(axis_at, blocks):
        steps = jax.random.uniform(jax.random.fold_in(jax.random.fold_in(own_key, 6), axis_at), (blocks,), jnp.float32, low / len(shards), largest / len(shards))
        return jnp.repeat(jnp.exp(steps), shape[axis_at] // blocks).reshape((-1,) + (1,) * (len(shape) - axis_at - 1))

    loudness = one(*shards[0])
    for cut in shards[1:]:
        loudness = loudness * one(*cut)
    return loudness


def centred(stream_key, dims, width, bound, pieces=(), kind=jnp.bfloat16):
    values = jax.random.normal(stream_key, dims, jnp.float32) * width
    if len(pieces) > 0:
        values = levels(stream_key, dims, pieces, -0.22, 0.18) * values
    return jnp.clip(values, min=-bound, max=bound).astype(kind)


def setup_inputs(seed: int = 0) -> dict:
    seeds = jax.random.split(jax.random.key(seed), 11)
    features = centred(seeds[0], (TOTAL, F), 1.0, 6.0, ((0, 32),))
    adjacency = centred(seeds[1], (DEVICES * BLK, BS, BS), (2 * BS) ** -0.5, 0.375, ((0, 32),))
    block_rows = draw_block_rows(jax.random.fold_in(seeds[10], 71), 0)
    block_cols = draw_block_cols(jax.random.fold_in(seeds[10], 71), 0)
    block_count = draw_block_count(jax.random.fold_in(seeds[10], 71), 0)
    node_count = draw_node_count(jax.random.fold_in(seeds[10], 71), 0)
    halo_index = draw_halo_index(jax.random.fold_in(seeds[10], 71), 0)
    weight = centred(seeds[7], (F, F), F ** -0.5, 0.25)
    bias = centred(seeds[8], (F,), 0.5, 3.0, (), jnp.float32)
    out_grad = centred(seeds[9], (TOTAL, F), 1.0, 6.0, ((0, 32),))
    return {"features": features, "adjacency": adjacency, "block_rows": block_rows, "block_cols": block_cols, "block_count": block_count, "node_count": node_count, "halo_index": halo_index, "weight": weight, "bias": bias, "out_grad": out_grad}


def device_pass(items, weight, bias):
    own, halos, blocks, rows, cols, count, keep, grads = items
    extended = jnp.concatenate([own, halos], 0).reshape(ECB, BS, F)
    live = jnp.arange(BLK) < count

    def forward_step(total, item):
        tile, row_id, col_id, alive = item
        prod = jnp.dot(tile, extended[col_id], preferred_element_type=jnp.float32)
        return (total.at[row_id].add(jnp.where(alive, prod, jnp.float32(0.0))), None)
    summed, _ = lax.scan(forward_step, jnp.zeros((RB, BS, F), jnp.float32), (blocks, rows, cols, live))
    aggregated = summed.reshape(NODE_DEV, F).astype(jnp.bfloat16)
    pre = jnp.dot(aggregated, weight, preferred_element_type=jnp.float32) + bias
    sig = jax.nn.sigmoid(pre)
    output = jnp.where(keep[:, None], pre * sig, jnp.float32(0.0)).astype(jnp.bfloat16)
    dpre = jnp.where(keep[:, None], grads.astype(jnp.float32) * sig * (1.0 + pre * (1.0 - sig)), jnp.float32(0.0)).astype(jnp.bfloat16)
    weight_part = jnp.dot(aggregated.T, dpre, preferred_element_type=jnp.float32)
    bias_part = lax.optimization_barrier(jnp.sum(dpre.astype(jnp.float32), 0))
    back = jnp.dot(dpre, weight.T, preferred_element_type=jnp.float32).astype(jnp.bfloat16).reshape(RB, BS, F)

    def backward_step(total, item):
        tile, row_id, col_id, alive = item
        prod = jnp.dot(tile.T, back[row_id], preferred_element_type=jnp.float32)
        return (total.at[col_id].add(jnp.where(alive, prod, jnp.float32(0.0))), None)
    spread, _ = lax.scan(backward_step, jnp.zeros((ECB, BS, F), jnp.float32), (blocks, rows, cols, live))
    own_part = spread[:RB].reshape(NODE_DEV, F)
    halo_part = spread[RB:].reshape(4, HALO, F).astype(jnp.bfloat16)
    return (output, weight_part, bias_part, own_part, halo_part)

def reference(features, adjacency, block_rows, block_cols, block_count, node_count, halo_index, weight, bias, out_grad):
    n_wide = N_WIDE
    n_narrow = N_NARROW
    feats = features.reshape(DEVICES, NODE_DEV, F)
    keep = jnp.arange(NODE_DEV)[None, :] < node_count[:, None]
    masked = jnp.where(keep[:, :, None], feats, jnp.zeros_like(feats))
    packed = jax.vmap(lambda rows_of, picks: rows_of[picks])(masked, halo_index)
    grid = packed.reshape(n_wide, n_narrow, 4, HALO, F)
    zero_wide = jnp.zeros((1, n_narrow, HALO, F), jnp.bfloat16)
    zero_narrow = jnp.zeros((n_wide, 1, HALO, F), jnp.bfloat16)
    seg_a = jnp.concatenate([zero_wide, grid[:-1, :, 1]], 0)
    seg_b = jnp.concatenate([grid[1:, :, 0], zero_wide], 0)
    seg_c = jnp.concatenate([zero_narrow, grid[:, :-1, 3]], 1)
    seg_d = jnp.concatenate([grid[:, 1:, 2], zero_narrow], 1)
    halos = jnp.stack([seg_a, seg_b, seg_c, seg_d], 2).reshape(DEVICES, 4 * HALO, F)
    blocks = adjacency.reshape(DEVICES, BLK, BS, BS)
    grads = out_grad.reshape(DEVICES, NODE_DEV, F)
    output, weight_parts, bias_parts, own_part, halo_part = lax.map(lambda items: device_pass(items, weight, bias), (masked, halos, blocks, block_rows, block_cols, block_count, keep, grads))
    scale = 1.0 / math.sqrt(TOTAL)
    weight_grad = lax.optimization_barrier(jnp.sum(weight_parts, 0)) * scale
    bias_grad = lax.optimization_barrier(jnp.sum(bias_parts, 0)) * scale
    hgrid = halo_part.astype(jnp.float32).reshape(n_wide, n_narrow, 4, HALO, F)
    fzero_wide = jnp.zeros((1, n_narrow, HALO, F), jnp.float32)
    fzero_narrow = jnp.zeros((n_wide, 1, HALO, F), jnp.float32)
    in_a = jnp.concatenate([fzero_wide, hgrid[:-1, :, 1]], 0)
    in_b = jnp.concatenate([hgrid[1:, :, 0], fzero_wide], 0)
    in_c = jnp.concatenate([fzero_narrow, hgrid[:, :-1, 3]], 1)
    in_d = jnp.concatenate([hgrid[:, 1:, 2], fzero_narrow], 1)
    incoming = jnp.stack([in_a, in_b, in_c, in_d], 2).reshape(DEVICES, 4 * HALO, F)
    summed = jax.vmap(lambda base, picks, extra: base.at[picks].add(extra))(own_part, halo_index.reshape(DEVICES, 4 * HALO), incoming)
    input_grad = jnp.where(keep[:, :, None], summed, jnp.float32(0.0)).astype(jnp.bfloat16)
    return (output.reshape(TOTAL, F), input_grad.reshape(TOTAL, F), weight_grad, bias_grad)
```

```python
import functools
import math

import jax
import jax.numpy as jnp
from jax import lax
from jax.experimental import pallas as pl
from jax.experimental.pallas import tpu as pltpu
from jax.sharding import PartitionSpec as P

MESH = pl.DeviceIdType.MESH
ANY = pl.ANY
VMEM_LIMIT = 60 * 1024 * 1024
FINISH_LIMIT = 60 * 1024 * 1024
BF = jnp.bfloat16
F32 = jnp.float32


def neighbours(n_wide, n_narrow):
    w = lax.axis_index("wide")
    n = lax.axis_index("narrow")
    return (
        (w > 0, (w - 1, n)),
        (w < n_wide - 1, (w + 1, n)),
        (n > 0, (w, n - 1)),
        (n < n_narrow - 1, (w, n + 1)),
    )


def halo_copy(src, dst, send, recv, k, target):
    return pltpu.make_async_remote_copy(
        src_ref=src.at[k],
        dst_ref=dst.at[k ^ 1],
        send_sem=send.at[k],
        recv_sem=recv.at[k ^ 1],
        device_id=target,
        device_id_type=MESH,
    )


def tables(row_ref, col_ref, pads, count, row_blocks, col_blocks):
    lanes = pads.shape[1]
    slots = row_ref.shape[1]
    halo_blocks = col_blocks - row_blocks
    pads[...] = jnp.zeros(pads.shape, pads.dtype)
    pads[0:1, 0:slots] = row_ref[...]
    pads[1:2, 0:slots] = col_ref[...]
    lane = lax.broadcasted_iota(jnp.int32, (lanes, lanes), 1)
    sub = lax.broadcasted_iota(jnp.int32, (lanes, lanes), 0)
    one = lambda m: jnp.where(m, 1, 0)
    spread = lambda x: jnp.broadcast_to(x, (lanes, lanes))
    down = lambda x: jnp.sum(x, 0, keepdims=True)
    across = lambda x: jnp.sum(x, 1, keepdims=True)

    row, col = spread(pads[0:1, :]), spread(pads[1:2, :])
    row_t, col_t = jnp.transpose(row), jnp.transpose(col)
    live = lane < count
    own = live & (col < row_blocks)
    own_t = (sub < count) & (col_t < row_blocks)
    before = own_t & (sub < lane)

    def first(a, a_t):
        return own & (spread(down(one(before & (a_t == a)))) == 0)

    def order(key):
        key_t = jnp.transpose(key)
        same = (key == key_t) & (lane < sub)
        rank = across(one((key < key_t) | same))
        twin = jnp.minimum(across(one(same)), 1)
        hot = one(jnp.broadcast_to(rank, (lanes, lanes)) == lane)
        return key_t, rank, twin, lambda x: down(hot * x)

    dead = 2 * col_blocks
    lead = first(row, row_t)
    key_t, rank, twin, pick = order(
        jnp.where(lead, row, jnp.where(live, row + row_blocks, dead))
    )
    at = lane + row_blocks
    has = down(one(key_t == at))
    last = jnp.where(has > 0, down(one(key_t <= at)) - 1, lane[0:1, :])
    prev = jnp.where(twin > 0, rank - 1, row_t)
    lines = [pick(sub), pick(col_t), pick(prev), last]

    lead = first(col, col_t)
    own_key = jnp.where(lead, col + (col_blocks + 1), col + halo_blocks)
    key = jnp.where(col < row_blocks, own_key, col - row_blocks)
    unused = jnp.where(lane < slots, col_blocks, dead)
    key_t, rank, twin, pick = order(jnp.where(live, key, unused))
    has = down(one(key_t == lane))
    ends = jnp.where(has > 0, down(one(key_t <= lane)), 0)
    keep = pick(jnp.broadcast_to(twin, (lanes, lanes)))
    lines += [pick(sub), pick(row_t), keep, ends]
    slot, block = slots - 1, row_blocks - 1
    tops = (slot, col_blocks - 1, slot, slot, slot, block, 1, slots - row_blocks)
    return [jnp.clip(line, 0, top) for line, top in zip(lines, tops)]


def layer_kernel(
    n_wide,
    n_narrow,
    scale,
    step,
    idx_ref,
    row_ref,
    col_ref,
    live,
    nodes_live,
    b_ref,
    feat_hbm,
    adj_hbm,
    grad_hbm,
    w_hbm,
    out_hbm,
    spread_hbm,
    incoming_hbm,
    wout_hbm,
    bout_hbm,
    grad,
    own_spread,
    incoming,
    wout_ref,
    bout_ref,
    pads,
    lined,
    table,
    ext,
    adj,
    w_ref,
    run,
    packed,
    landing,
    ret,
    wsum,
    wg,
    bsum,
    bg,
    rs_wide,
    rs_narrow,
    part,
    ag_narrow,
    ag_wide,
    b_wide,
    b_mid,
    b_narrow,
    load,
    out_sem,
    own_sem,
    give,
    send,
    recv,
    send_r,
    recv_r,
    send_w,
    recv_w,
    send_n,
    recv_n,
    send_gn,
    recv_gn,
    send_gw,
    recv_gw,
    send_bw,
    recv_bw,
    send_bn,
    recv_bn,
):
    w = lax.axis_index("wide")
    n = lax.axis_index("narrow")
    slots = adj.shape[0]
    row_blocks, side, width = feat_hbm.shape
    col_blocks = ext.shape[0]
    halo_blocks = col_blocks - row_blocks
    half = row_blocks // 2
    count = idx_ref.shape[2]
    per = count // side
    slab = rs_wide.shape[1]
    part_width = rs_narrow.shape[2]
    keep_to = nodes_live[0]

    loads = [
        pltpu.make_async_copy(feat_hbm.at[pl.ds(0, half)], ext.at[pl.ds(0, half)], load.at[0]),
        pltpu.make_async_copy(feat_hbm.at[pl.ds(half, half)], ext.at[pl.ds(half, half)], load.at[1]),
        pltpu.make_async_copy(adj_hbm, adj, load.at[2]),
        pltpu.make_async_copy(w_hbm, w_ref, load.at[3]),
        pltpu.make_async_copy(grad_hbm, grad, load.at[4]),
    ]
    for fetch in loads:
        fetch.start()

    def wide_peer(d):
        return (lax.rem(w + d, n_wide), n)

    def narrow_peer(d):
        return (w, lax.rem(n + d, n_narrow))

    def remote(src, dst, s, r, peer):
        return pltpu.make_async_remote_copy(
            src_ref=src, dst_ref=dst, send_sem=s, recv_sem=r, device_id=peer, device_id_type=MESH
        )

    near = neighbours(n_wide, n_narrow)
    peers = [wide_peer(d) for d in range(1, n_wide)] + [
        narrow_peer(d) for d in range(1, n_narrow)
    ]
    barrier = pltpu.get_barrier_semaphore()
    for peer in peers:
        pl.semaphore_signal(barrier, inc=1, device_id=peer, device_id_type=MESH)

    for i, line in enumerate(tables(row_ref, col_ref, pads, live[0], row_blocks, col_blocks)):
        lined[pl.ds(i, 1), :] = line
    tabled = pltpu.make_async_copy(lined, table, load.at[5])
    tabled.start()

    ext[pl.ds(row_blocks, halo_blocks)] = jnp.zeros((halo_blocks, side, width), BF)
    wsum[...] = jnp.zeros_like(wsum)
    bsum[...] = jnp.zeros_like(bsum)
    loads[0].wait()
    span = half * side
    lane = lax.broadcasted_iota(jnp.int32, (count, 128), 1).astype(F32)

    def pack(k):
        row = idx_ref[0, pl.ds(k, 1), :].astype(F32)
        column = jnp.transpose(jnp.broadcast_to(row, (128, count)))
        hot = jnp.concatenate(
            [jnp.where(column == lane + float(at), 1.0, 0.0).astype(BF) for at in range(0, span, 128)],
            axis=1,
        )
        near_rows = ext[pl.ds(0, half)].reshape(span, width)
        packed[k] = jnp.dot(hot, near_rows, preferred_element_type=F32).astype(BF)

    pack(2)
    pl.semaphore_wait(barrier, len(peers))
    for k in (2, 3, 1, 0):
        there, target = near[k]
        if k != 2:
            pack(k)

        @pl.when(there)
        def _():
            halo_copy(packed, landing, send, recv, k, target).start()

    def kept(block, blocks=1):
        at = lax.broadcasted_iota(jnp.int32, (blocks * side, width), 0)
        return at < keep_to - block * side

    loads[1].wait()

    def mask(i, carry):
        ext[i] = jnp.where(kept(i), ext[i].astype(F32), 0.0).astype(BF)
        return carry

    lax.fori_loop(half, row_blocks, mask, 0)
    loads[2].wait()
    tabled.wait()

    def product(k):
        return jnp.dot(adj[table[0, k]], ext[table[1, k]], preferred_element_type=F32)

    unroll = 16

    def leading(t, carry):
        for u in range(unroll):
            k = t * unroll + u
            run[k] = product(k)
        return carry

    lax.fori_loop(0, row_blocks // unroll, leading, 0)
    for k in (1, 0, 2, 3):
        there, target = near[k]

        @pl.when(there)
        def _():
            halo_copy(packed, landing, send, recv, k, target).wait_send()
            halo_copy(packed, landing, send, recv, k ^ 1, target).wait_recv()
            ext[pl.ds(row_blocks + k * per, per)] = landing[k].reshape(per, side, width)

    def following(t, carry):
        for u in range(unroll):
            k = t * unroll + u
            run[k] = run[table[2, k]] + product(k)
        return carry

    lax.fori_loop(row_blocks // unroll, slots // unroll, following, 0)
    loads[3].wait()
    loads[4].wait()

    tall = step * side

    def put(i):
        at = pl.ds(i * step, step)
        return pltpu.make_async_copy(grad.at[at], out_hbm.at[at], out_sem.at[i])

    def put_own(t):
        at = pl.ds(t * unroll, unroll)
        return pltpu.make_async_copy(own_spread.at[at], spread_hbm.at[at], own_sem.at[t])

    def into(i):
        agg = jnp.concatenate([run[table[3, i * step + j]] for j in range(step)], 0).astype(BF)
        return agg, jnp.dot(agg, w_ref[...], preferred_element_type=F32)

    def middle(i, pre):
        at = pl.ds(i * step, step)
        g = grad[at].reshape(tall, width).astype(F32)
        pre = pre + b_ref[...]
        keep = kept(i * step, step)
        sig = 0.5 * jnp.tanh(0.5 * pre) + 0.5
        act = pre * sig
        grad[at] = jnp.where(keep, act, 0.0).astype(BF).reshape(step, side, width)
        put(i).start()
        dpre = jnp.where(keep, g * (sig + act * (1.0 - sig)), 0.0).astype(BF)
        bsum[...] += jnp.sum(dpre.astype(F32).reshape(tall // 8, 8, width), 0)
        return dpre

    def after(i, agg, dpre):
        wsum[...] += lax.dot_general(
            agg, dpre, (((0,), (0,)), ((), ())), preferred_element_type=F32
        )
        ext[pl.ds(i * step, step)] = (
            lax.dot_general(dpre, w_ref[...], (((1,), (1,)), ((), ())), preferred_element_type=F32)
            .astype(BF)
            .reshape(step, side, width)
        )

    group = 8

    def dense(t, carry):
        now = into(t * group)
        for u in range(group):
            i = t * group + u
            later = into(i + 1) if u + 1 < group else None
            dpre = middle(i, now[1])
            after(i, now[0], dpre)
            now = later
        return carry

    lax.fori_loop(0, row_blocks // step // group, dense, 0)
    wg[...] = wsum[...].astype(BF).reshape(n_wide, slab, width)
    bg[...] = jnp.sum(bsum[...], 0, keepdims=True)

    first = []
    for d in range(1, n_wide):
        peer = wide_peer(d)
        c = remote(wg.at[peer[0]], rs_wide.at[d], send_w.at[d], recv_w.at[d], peer)
        c.start()
        first.append(c)
    bias_first = []
    for d in range(1, n_wide):
        c = remote(bg, b_wide.at[d], send_bw.at[d], recv_bw.at[d], wide_peer(d))
        c.start()
        bias_first.append(c)
    run[0] = jnp.zeros(run.shape[1:], run.dtype)

    def spreading(k):
        return lax.dot_general(
            adj[table[4, k]], ext[table[5, k]], (((0,), (0,)), ((), ())), preferred_element_type=F32
        )

    def backward(t, carry):
        held = run[t * unroll]
        for u in range(unroll):
            k = t * unroll + u
            held = held * table[6, k].astype(F32) + spreading(k)
            run[k + 1] = held
        return carry

    early = slots - row_blocks
    lax.fori_loop(0, early // unroll, backward, 0)
    for k in (2, 3, 1, 0):
        there, target = near[k]
        for j in range(per):
            ret[k, pl.ds(j * side, side), :] = run[table[7, k * per + j]].astype(BF)

        @pl.when(there)
        def _():
            halo_copy(ret, incoming, send_r, recv_r, k, target).start()

        @pl.when(jnp.logical_not(there))
        def _():
            incoming[k] = jnp.zeros(incoming.shape[1:], BF)

    total = wg[w].astype(F32)
    for c in first:
        c.wait_recv()
    for d in range(1, n_wide):
        total = total + rs_wide[d].astype(F32)
    bias = bg[...]
    for c in bias_first:
        c.wait_recv()
    for d in range(1, n_wide):
        bias = bias + b_wide[d]
    b_mid[...] = bias
    for j in range(n_narrow):
        part[j] = total[:, j * part_width : (j + 1) * part_width].astype(BF)
    second = []
    for d in range(1, n_narrow):
        peer = narrow_peer(d)
        c = remote(part.at[peer[1]], rs_narrow.at[d], send_n.at[d], recv_n.at[d], peer)
        c.start()
        second.append(c)
    for d in range(1, n_narrow):
        c = remote(b_mid, b_narrow.at[d], send_bn.at[d], recv_bn.at[d], narrow_peer(d))
        c.start()
        bias_first.append(c)
        second.append(c)

    def own(c):
        return run[table[7, halo_blocks + c]] + spreading(early + c)

    def low(t, carry):
        for u in range(unroll):
            c = t * unroll + u
            own_spread[c] = own(c).astype(BF)
        put_own(t).start()
        return carry

    lax.fori_loop(0, half // unroll, low, 0)
    piece = part[n].astype(F32)
    for c in second:
        c.wait_recv()
    for d in range(1, n_narrow):
        piece = piece + rs_narrow[d].astype(F32)
        bias = bias + b_narrow[d]
    bout_ref[...] = bias * scale
    ag_narrow[n] = (piece * scale).astype(BF)
    third = []
    for d in range(1, n_narrow):
        c = remote(ag_narrow.at[n], ag_narrow.at[n], send_gn.at[d], recv_gn.at[d], narrow_peer(d))
        c.start()
        third.append(c)

    def high(t, carry):
        for u in range(unroll):
            c = t * unroll + u
            own_spread[c] = jnp.where(kept(c), own(c), 0.0).astype(BF)
        put_own(t).start()
        return carry

    lax.fori_loop(half // unroll, row_blocks // unroll, high, 0)
    for c in third:
        c.wait_recv()
    fourth = []
    for d in range(1, n_wide):
        c = remote(ag_narrow, ag_wide.at[w], send_gw.at[d], recv_gw.at[d], wide_peer(d))
        c.start()
        fourth.append(c)
    ag_wide[w] = ag_narrow[...]
    for k in range(4):
        there, target = near[k]

        @pl.when(there)
        def _():
            halo_copy(ret, incoming, send_r, recv_r, k, target).wait_send()
            halo_copy(ret, incoming, send_r, recv_r, k ^ 1, target).wait_recv()

    gives = [
        pltpu.make_async_copy(incoming, incoming_hbm, give.at[0]),
        pltpu.make_async_copy(wout_ref, wout_hbm, give.at[1]),
        pltpu.make_async_copy(bout_ref, bout_hbm, give.at[2]),
    ]
    gives[0].start()
    for c in fourth:
        c.wait_recv()
    for i in range(n_wide):
        for j in range(n_narrow):
            wout_ref[pl.ds(i * slab, slab), pl.ds(j * part_width, part_width)] = ag_wide[
                i, j
            ].astype(F32)
    for c in gives[1:]:
        c.start()

    def drain(i, carry):
        put(i).wait()
        return carry

    lax.fori_loop(0, row_blocks // step, drain, 0)
    for t in range(row_blocks // unroll):
        put_own(t).wait()
    for c in gives:
        c.wait()
    for c in first + bias_first + second[: n_narrow - 1] + third + fourth:
        c.wait_send()


def finish_kernel(
    idx_ref,
    spread_hbm,
    incoming_hbm,
    out_in,
    w_in,
    b_in,
    grad_hbm,
    out_hbm,
    w_hbm,
    b_hbm,
    grad,
    incoming,
    out,
    wg,
    bg,
    take,
    give,
    first_take,
):
    chunks, chunk, width = grad.shape
    half = chunks // 2
    heads = [
        pltpu.make_async_copy(incoming_hbm, incoming, first_take.at[0]),
        pltpu.make_async_copy(
            spread_hbm.at[pl.ds(0, half)], grad.at[pl.ds(0, half)], first_take.at[1]
        ),
    ]
    hops = [(out_in.at[i], out.at[i], out_hbm.at[i]) for i in range(out.shape[0])]
    hops += [(spread_hbm.at[i], grad.at[i], grad_hbm.at[i]) for i in range(half, chunks)]
    hops += [(w_in, wg, w_hbm), (b_in, bg, b_hbm)]
    ins = [pltpu.make_async_copy(a, b, take.at[i]) for i, (a, b, _) in enumerate(hops)]
    outs = [pltpu.make_async_copy(b, c, give.at[i]) for i, (_, b, c) in enumerate(hops)]
    for c in heads + ins:
        c.start()
    idx = jnp.concatenate([idx_ref[0, k : k + 1, :] for k in range(incoming.shape[0])], 1)
    for c in heads:
        c.wait()
    merged = incoming[...].reshape(-1, width)
    per = -(-len(hops) // half)
    for i in range(half):
        row = lax.broadcasted_iota(jnp.int32, (chunk, idx.shape[1]), 0) + i * chunk
        hot = jnp.where(row == idx, 1.0, 0.0).astype(BF)
        full = grad[i].astype(F32) + jnp.dot(hot, merged, preferred_element_type=F32)
        grad[i] = full.astype(BF)
        c = pltpu.make_async_copy(grad.at[i], grad_hbm.at[i], give.at[len(hops) + i])
        c.start()
        outs.append(c)
        for j in range(i * per, min(i * per + per, len(hops))):
            ins[j].wait()
            outs[j].start()
    for c in outs:
        c.wait()


def local(
    n_wide,
    n_narrow,
    features,
    adjacency,
    block_rows,
    block_cols,
    block_count,
    node_count,
    halo_index,
    weight,
    bias,
    out_grad,
):
    nodes, width = features.shape
    slots, side, _ = adjacency.shape
    row_blocks = nodes // side
    sides, halo = halo_index.shape[1:]
    halo_blocks = sides * halo // side
    col_blocks = row_blocks + halo_blocks
    vm = pl.BlockSpec(memory_space=pltpu.VMEM)
    sm = pl.BlockSpec(memory_space=pltpu.SMEM)
    hb = pl.BlockSpec(memory_space=ANY)
    dma = pltpu.SemaphoreType.DMA
    shape = jax.ShapeDtypeStruct
    blocked = (row_blocks, side, width)
    lanes = -(-slots // 128) * 128
    slab = width // n_wide
    part_width = width // n_narrow
    scale = 1.0 / math.sqrt(nodes * n_wide * n_narrow)
    step = 2
    chunk = 2 * side
    chunked = (nodes // chunk, chunk, width)
    pieces = 8
    pieced = (pieces, nodes // pieces, width)
    hops = pieces + nodes // chunk // 2 + 2
    out, own_spread, incoming, wout, bout = pl.pallas_call(
        functools.partial(layer_kernel, n_wide, n_narrow, scale, step),
        name="layer",
        out_shape=(
            shape(blocked, BF),
            shape(blocked, BF),
            shape((sides, halo, width), BF),
            shape((width, width), F32),
            shape((1, width), F32),
        ),
        in_specs=[vm, vm, vm, sm, sm, vm, hb, hb, hb, hb],
        out_specs=(hb,) * 5,
        scratch_shapes=[
            pltpu.VMEM(blocked, BF),
            pltpu.VMEM(blocked, BF),
            pltpu.VMEM((sides, halo, width), BF),
            pltpu.VMEM((width, width), F32),
            pltpu.VMEM((1, width), F32),
            pltpu.VMEM((8, lanes), jnp.int32),
            pltpu.VMEM((8, lanes), jnp.int32),
            pltpu.SMEM((8, lanes), jnp.int32),
            pltpu.VMEM((col_blocks, side, width), BF),
            pltpu.VMEM((slots, side, side), BF),
            pltpu.VMEM((width, width), BF),
            pltpu.VMEM((slots, side, width), F32),
            pltpu.VMEM((sides, halo, width), BF),
            pltpu.VMEM((sides, halo, width), BF),
            pltpu.VMEM((sides, halo, width), BF),
            pltpu.VMEM((width, width), F32),
            pltpu.VMEM((n_wide, slab, width), BF),
            pltpu.VMEM((8, width), F32),
            pltpu.VMEM((1, width), F32),
            pltpu.VMEM((n_wide, slab, width), BF),
            pltpu.VMEM((n_narrow, slab, part_width), BF),
            pltpu.VMEM((n_narrow, slab, part_width), BF),
            pltpu.VMEM((n_narrow, slab, part_width), BF),
            pltpu.VMEM((n_wide, n_narrow, slab, part_width), BF),
            pltpu.VMEM((n_wide, 1, width), F32),
            pltpu.VMEM((1, width), F32),
            pltpu.VMEM((n_narrow, 1, width), F32),
            dma((6,)),
            dma((row_blocks // step,)),
            dma((row_blocks,)),
            dma((3,)),
        ]
        + [dma((sides,))] * 4
        + [dma((n_wide,))] * 2
        + [dma((n_narrow,))] * 4
        + [dma((n_wide,))] * 4
        + [dma((n_narrow,))] * 2,
        compiler_params=pltpu.CompilerParams(
            collective_id=0, has_side_effects=True, vmem_limit_bytes=VMEM_LIMIT
        ),
    )(
        halo_index,
        block_rows,
        block_cols,
        block_count,
        node_count,
        bias.reshape(1, width),
        features.reshape(blocked),
        adjacency,
        out_grad.reshape(blocked),
        weight,
    )
    input_grad, out, wout, bout = pl.pallas_call(
        finish_kernel,
        name="finish",
        out_shape=(
            shape(chunked, BF),
            shape(pieced, BF),
            shape((width, width), F32),
            shape((1, width), F32),
        ),
        in_specs=[vm, hb, hb, hb, hb, hb],
        out_specs=(hb, hb, hb, hb),
        scratch_shapes=[
            pltpu.VMEM(chunked, BF),
            pltpu.VMEM((sides, halo, width), BF),
            pltpu.VMEM(pieced, BF),
            pltpu.VMEM((width, width), F32),
            pltpu.VMEM((1, width), F32),
            dma((hops,)),
            dma((hops + nodes // chunk // 2,)),
            dma((2,)),
        ],
        compiler_params=pltpu.CompilerParams(vmem_limit_bytes=FINISH_LIMIT),
    )(halo_index, own_spread.reshape(chunked), incoming, out.reshape(pieced), wout, bout)
    return out.reshape(nodes, width), input_grad.reshape(nodes, width), wout, bout.reshape(width)


def solution(mesh):
    both = ("wide", "narrow")
    placed = (
        P(both, None),
        P(both, None, None),
        P(both, None),
        P(both, None),
        P(both),
        P(both),
        P(both, None, None),
        P(),
        P(),
        P(both, None),
    )
    return jax.shard_map(
        functools.partial(local, mesh.shape["wide"], mesh.shape["narrow"]),
        mesh=mesh,
        in_specs=placed,
        out_specs=(P(both, None), P(both, None), P(), P()),
        check_vma=False,
    )
```

```python
import functools
import math

import jax
import jax.numpy as jnp
from jax import lax
from jax.experimental import pallas as pl
from jax.experimental.pallas import tpu as pltpu
from jax.sharding import PartitionSpec as P

MESH = pl.DeviceIdType.MESH
ANY = pl.ANY
VMEM_LIMIT = 48 * 1024 * 1024
FINISH_LIMIT = 16 * 1024 * 1024
BF = jnp.bfloat16
F32 = jnp.float32


def neighbours(n_wide, n_narrow):
    w = lax.axis_index("wide")
    n = lax.axis_index("narrow")
    return (
        (w > 0, (w - 1, n)),
        (w < n_wide - 1, (w + 1, n)),
        (n > 0, (w, n - 1)),
        (n < n_narrow - 1, (w, n + 1)),
    )


def halo_copy(src, dst, send, recv, k, target):
    return pltpu.make_async_remote_copy(
        src_ref=src.at[k],
        dst_ref=dst.at[k ^ 1],
        send_sem=send.at[k],
        recv_sem=recv.at[k ^ 1],
        device_id=target,
        device_id_type=MESH,
    )


def tables(row_ref, col_ref, pads, count, row_blocks, col_blocks):
    lanes = pads.shape[1]
    slots = row_ref.shape[1]
    halo_blocks = col_blocks - row_blocks
    pads[...] = jnp.zeros(pads.shape, pads.dtype)
    pads[0:1, 0:slots] = row_ref[...]
    pads[1:2, 0:slots] = col_ref[...]
    lane = lax.broadcasted_iota(jnp.int32, (lanes, lanes), 1)
    sub = lax.broadcasted_iota(jnp.int32, (lanes, lanes), 0)
    one = lambda m: jnp.where(m, 1, 0)
    spread = lambda x: jnp.broadcast_to(x, (lanes, lanes))
    down = lambda x: jnp.sum(x, 0, keepdims=True)
    across = lambda x: jnp.sum(x, 1, keepdims=True)

    row, col = spread(pads[0:1, :]), spread(pads[1:2, :])
    row_t, col_t = jnp.transpose(row), jnp.transpose(col)
    live = lane < count
    own = live & (col < row_blocks)
    own_t = (sub < count) & (col_t < row_blocks)
    before = own_t & (sub < lane)

    def first(a, a_t):
        return own & (spread(down(one(before & (a_t == a)))) == 0)

    def order(key):
        key_t = jnp.transpose(key)
        same = (key == key_t) & (lane < sub)
        rank = across(one((key < key_t) | same))
        twin = jnp.minimum(across(one(same)), 1)
        hot = one(jnp.broadcast_to(rank, (lanes, lanes)) == lane)
        return key_t, rank, twin, lambda x: down(hot * x)

    dead = 2 * col_blocks
    lead = first(row, row_t)
    key_t, rank, twin, pick = order(
        jnp.where(lead, row, jnp.where(live, row + row_blocks, dead))
    )
    at = lane + row_blocks
    has = down(one(key_t == at))
    last = jnp.where(has > 0, down(one(key_t <= at)) - 1, lane[0:1, :])
    prev = jnp.where(twin > 0, rank - 1, row_t)
    lines = [pick(sub), pick(col_t), pick(prev), last]

    lead = first(col, col_t)
    own_key = jnp.where(lead, col + (col_blocks + 1), col + halo_blocks)
    key = jnp.where(col < row_blocks, own_key, col - row_blocks)
    unused = jnp.where(lane < slots, col_blocks, dead)
    key_t, rank, twin, pick = order(jnp.where(live, key, unused))
    has = down(one(key_t == lane))
    ends = jnp.where(has > 0, down(one(key_t <= lane)), 0)
    keep = pick(jnp.broadcast_to(twin, (lanes, lanes)))
    lines += [pick(sub), pick(row_t), keep, ends]
    slot, block = slots - 1, row_blocks - 1
    tops = (slot, col_blocks - 1, slot, slot, slot, block, 1, slots - row_blocks)
    return [jnp.clip(line, 0, top) for line, top in zip(lines, tops)]


def layer_kernel(
    n_wide,
    n_narrow,
    scale,
    step,
    idx_ref,
    row_ref,
    col_ref,
    live,
    nodes_live,
    b_ref,
    feat_hbm,
    adj_hbm,
    grad_hbm,
    w_hbm,
    grad,
    own_spread,
    incoming,
    ag_wide,
    bout_ref,
    pads,
    lined,
    table,
    ext,
    adj,
    w_ref,
    run,
    packed,
    landing,
    ret,
    wsum,
    wg,
    bsum,
    bg,
    rs_wide,
    rs_narrow,
    part,
    ag_narrow,
    b_wide,
    b_mid,
    b_narrow,
    load,
    send,
    recv,
    send_r,
    recv_r,
    send_w,
    recv_w,
    send_n,
    recv_n,
    send_gn,
    recv_gn,
    send_gw,
    recv_gw,
    send_bw,
    recv_bw,
    send_bn,
    recv_bn,
):
    w = lax.axis_index("wide")
    n = lax.axis_index("narrow")
    slots = adj.shape[0]
    row_blocks, side, width = feat_hbm.shape
    col_blocks = ext.shape[0]
    halo_blocks = col_blocks - row_blocks
    half = row_blocks // 2
    count = idx_ref.shape[2]
    per = count // side
    slab = rs_wide.shape[1]
    part_width = rs_narrow.shape[2]
    keep_to = nodes_live[0]

    loads = [
        pltpu.make_async_copy(feat_hbm.at[pl.ds(0, half)], ext.at[pl.ds(0, half)], load.at[0]),
        pltpu.make_async_copy(feat_hbm.at[pl.ds(half, half)], ext.at[pl.ds(half, half)], load.at[1]),
        pltpu.make_async_copy(adj_hbm, adj, load.at[2]),
        pltpu.make_async_copy(w_hbm, w_ref, load.at[3]),
        pltpu.make_async_copy(grad_hbm, grad, load.at[4]),
    ]
    for fetch in loads:
        fetch.start()

    def wide_peer(d):
        return (lax.rem(w + d, n_wide), n)

    def narrow_peer(d):
        return (w, lax.rem(n + d, n_narrow))

    def remote(src, dst, s, r, peer):
        return pltpu.make_async_remote_copy(
            src_ref=src, dst_ref=dst, send_sem=s, recv_sem=r, device_id=peer, device_id_type=MESH
        )

    near = neighbours(n_wide, n_narrow)
    peers = [wide_peer(d) for d in range(1, n_wide)] + [
        narrow_peer(d) for d in range(1, n_narrow)
    ]
    barrier = pltpu.get_barrier_semaphore()
    for peer in peers:
        pl.semaphore_signal(barrier, inc=1, device_id=peer, device_id_type=MESH)

    for i, line in enumerate(tables(row_ref, col_ref, pads, live[0], row_blocks, col_blocks)):
        lined[pl.ds(i, 1), :] = line
    tabled = pltpu.make_async_copy(lined, table, load.at[5])
    tabled.start()

    ext[pl.ds(row_blocks, halo_blocks)] = jnp.zeros((halo_blocks, side, width), BF)
    wsum[...] = jnp.zeros_like(wsum)
    bsum[...] = jnp.zeros_like(bsum)
    loads[0].wait()
    span = half * side
    lane = lax.broadcasted_iota(jnp.int32, (count, 128), 1).astype(F32)

    def pack(k):
        row = idx_ref[0, pl.ds(k, 1), :].astype(F32)
        column = jnp.transpose(jnp.broadcast_to(row, (128, count)))
        hot = jnp.concatenate(
            [jnp.where(column == lane + float(at), 1.0, 0.0).astype(BF) for at in range(0, span, 128)],
            axis=1,
        )
        near_rows = ext[pl.ds(0, half)].reshape(span, width)
        packed[k] = jnp.dot(hot, near_rows, preferred_element_type=F32).astype(BF)

    pack(2)
    pl.semaphore_wait(barrier, len(peers))
    for k in (2, 3, 1, 0):
        there, target = near[k]
        if k != 2:
            pack(k)

        @pl.when(there)
        def _():
            halo_copy(packed, landing, send, recv, k, target).start()

    def kept(block, blocks=1):
        at = lax.broadcasted_iota(jnp.int32, (blocks * side, width), 0)
        return at < keep_to - block * side

    loads[1].wait()

    def mask(i, carry):
        ext[i] = jnp.where(kept(i), ext[i].astype(F32), 0.0).astype(BF)
        return carry

    lax.fori_loop(half, row_blocks, mask, 0)
    loads[2].wait()
    tabled.wait()

    def product(k):
        return jnp.dot(adj[table[0, k]], ext[table[1, k]], preferred_element_type=F32)

    unroll = 16

    def leading(t, carry):
        for u in range(unroll):
            k = t * unroll + u
            run[k] = product(k)
        return carry

    lax.fori_loop(0, row_blocks // unroll, leading, 0)
    for k in (1, 0, 2, 3):
        there, target = near[k]

        @pl.when(there)
        def _():
            halo_copy(packed, landing, send, recv, k, target).wait_send()
            halo_copy(packed, landing, send, recv, k ^ 1, target).wait_recv()
            ext[pl.ds(row_blocks + k * per, per)] = landing[k].reshape(per, side, width)

    def following(t, carry):
        for u in range(unroll):
            k = t * unroll + u
            run[k] = run[table[2, k]] + product(k)
        return carry

    lax.fori_loop(row_blocks // unroll, slots // unroll, following, 0)
    loads[3].wait()
    loads[4].wait()

    tall = step * side

    def into(i):
        agg = jnp.concatenate([run[table[3, i * step + j]] for j in range(step)], 0).astype(BF)
        return agg, jnp.dot(agg, w_ref[...], preferred_element_type=F32)

    def middle(i, pre):
        at = pl.ds(i * step, step)
        g = grad[at].reshape(tall, width).astype(F32)
        pre = pre + b_ref[...]
        keep = kept(i * step, step)
        sig = 0.5 * jnp.tanh(0.5 * pre) + 0.5
        act = pre * sig
        grad[at] = jnp.where(keep, act, 0.0).astype(BF).reshape(step, side, width)
        dpre = jnp.where(keep, g * (sig + act * (1.0 - sig)), 0.0).astype(BF)
        bsum[...] += jnp.sum(dpre.astype(F32).reshape(tall // 8, 8, width), 0)
        return dpre

    def after(i, agg, dpre):
        wsum[...] += lax.dot_general(
            agg, dpre, (((0,), (0,)), ((), ())), preferred_element_type=F32
        )
        ext[pl.ds(i * step, step)] = dpre.reshape(step, side, width)

    group = 8

    def dense(t, carry):
        now = into(t * group)
        for u in range(group):
            i = t * group + u
            later = into(i + 1) if u + 1 < group else None
            dpre = middle(i, now[1])
            after(i, now[0], dpre)
            now = later
        return carry

    lax.fori_loop(0, row_blocks // step // group, dense, 0)
    wg[...] = wsum[...].astype(BF).reshape(n_wide, slab, width)
    bg[...] = jnp.sum(bsum[...], 0, keepdims=True)

    first = []
    for d in range(1, n_wide):
        peer = wide_peer(d)
        c = remote(wg.at[peer[0]], rs_wide.at[d], send_w.at[d], recv_w.at[d], peer)
        c.start()
        first.append(c)
    bias_first = []
    for d in range(1, n_wide):
        c = remote(bg, b_wide.at[d], send_bw.at[d], recv_bw.at[d], wide_peer(d))
        c.start()
        bias_first.append(c)
    run[0] = jnp.zeros(run.shape[1:], run.dtype)
    deep = 8

    def backed(t, carry):
        at = pl.ds(t * deep, deep)
        ext[at] = (
            lax.dot_general(
                ext[at].reshape(deep * side, width),
                w_ref[...],
                (((1,), (1,)), ((), ())),
                preferred_element_type=F32,
            )
            .astype(BF)
            .reshape(deep, side, width)
        )
        return carry

    lax.fori_loop(0, row_blocks // deep, backed, 0)

    def spreading(k):
        return lax.dot_general(
            adj[table[4, k]], ext[table[5, k]], (((0,), (0,)), ((), ())), preferred_element_type=F32
        )

    def backward(t, carry):
        held = run[t * unroll]
        for u in range(unroll):
            k = t * unroll + u
            held = held * table[6, k].astype(F32) + spreading(k)
            run[k + 1] = held
        return carry

    early = slots - row_blocks
    lax.fori_loop(0, early // unroll, backward, 0)
    total = wg[w].astype(F32)
    for c in first:
        c.wait_recv()
    for d in range(1, n_wide):
        total = total + rs_wide[d].astype(F32)
    bias = bg[...]
    for c in bias_first:
        c.wait_recv()
    for d in range(1, n_wide):
        bias = bias + b_wide[d]
    b_mid[...] = bias
    for j in range(n_narrow):
        part[j] = total[:, j * part_width : (j + 1) * part_width].astype(BF)
    second = []
    for d in range(1, n_narrow):
        peer = narrow_peer(d)
        c = remote(part.at[peer[1]], rs_narrow.at[d], send_n.at[d], recv_n.at[d], peer)
        c.start()
        second.append(c)
    for d in range(1, n_narrow):
        c = remote(b_mid, b_narrow.at[d], send_bn.at[d], recv_bn.at[d], narrow_peer(d))
        c.start()
        bias_first.append(c)
        second.append(c)

    def returned(k, j):
        at = pl.ds(j * side, side)
        return pltpu.make_async_remote_copy(
            src_ref=ret.at[k, at],
            dst_ref=incoming.at[k ^ 1, at],
            send_sem=send_r.at[k, j],
            recv_sem=recv_r.at[k ^ 1, j],
            device_id=near[k][1],
            device_id_type=MESH,
        )

    def give_back(k, j):
        ret[k, pl.ds(j * side, side), :] = run[table[7, k * per + j]].astype(BF)

        @pl.when(near[k][0])
        def _():
            returned(k, j).start()

        @pl.when(jnp.logical_not(near[k][0]))
        def _():
            incoming[k, pl.ds(j * side, side), :] = jnp.zeros((side, width), BF)

    early_return = [(k, j) for k in (2, 3) for j in range(per // 2)]
    early_return += [(k, j) for k in (1, 0) for j in range(per)]
    for k, j in early_return:
        give_back(k, j)

    def own(c):
        return run[table[7, halo_blocks + c]] + spreading(early + c)

    def low(t, carry):
        for u in range(unroll):
            c = t * unroll + u
            own_spread[c] = own(c).astype(BF)
        return carry

    lax.fori_loop(0, half // unroll, low, 0)
    piece = part[n].astype(F32)
    for c in second:
        c.wait_recv()
    for d in range(1, n_narrow):
        piece = piece + rs_narrow[d].astype(F32)
        bias = bias + b_narrow[d]
    bout_ref[...] = bias * scale
    ag_narrow[n] = (piece * scale).astype(BF)
    third = []
    for d in range(1, n_narrow):
        c = remote(ag_narrow.at[n], ag_narrow.at[n], send_gn.at[d], recv_gn.at[d], narrow_peer(d))
        c.start()
        third.append(c)
    for k in (2, 3):
        for j in range(per // 2, per):
            give_back(k, j)

    def high(t, carry):
        for u in range(unroll):
            c = t * unroll + u
            own_spread[c] = jnp.where(kept(c), own(c), 0.0).astype(BF)
        return carry

    lax.fori_loop(half // unroll, row_blocks // unroll, high, 0)
    for c in third:
        c.wait_recv()
    fourth = []
    for d in range(1, n_wide):
        c = remote(ag_narrow, ag_wide.at[w], send_gw.at[d], recv_gw.at[d], wide_peer(d))
        c.start()
        fourth.append(c)
    ag_wide[w] = ag_narrow[...]
    for k in range(4):
        there, target = near[k]

        @pl.when(there)
        def _():
            for j in range(per):
                returned(k, j).wait_send()
                returned(k ^ 1, j).wait_recv()

    for c in fourth:
        c.wait_recv()
    for c in first + bias_first + second[: n_narrow - 1] + third + fourth:
        c.wait_send()


def finish_kernel(
    idx_ref,
    spread_ref,
    incoming,
    out_ref,
    ag_wide,
    b_ref,
    grad_hbm,
    out_hbm,
    w_hbm,
    b_hbm,
    grad,
    wg,
    give,
    part_give,
):
    half, chunk, width = grad.shape
    n_wide, n_narrow, slab, part_width = ag_wide.shape
    moves = [
        pltpu.make_async_copy(out_ref, out_hbm, give.at[0]),
        pltpu.make_async_copy(
            spread_ref.at[pl.ds(half, half)], grad_hbm.at[pl.ds(half, half)], give.at[1]
        ),
        pltpu.make_async_copy(b_ref, b_hbm, give.at[2]),
    ]
    for c in moves:
        c.start()
    for i in range(n_wide):
        for j in range(n_narrow):
            wg[pl.ds(i * slab, slab), pl.ds(j * part_width, part_width)] = ag_wide[i, j].astype(F32)
    moves.append(pltpu.make_async_copy(wg, w_hbm, give.at[3]))
    moves[3].start()
    merged = incoming[...].reshape(-1, width)
    idx = jnp.concatenate([idx_ref[0, k : k + 1, :] for k in range(incoming.shape[0])], 1)

    def leave(i):
        return pltpu.make_async_copy(grad.at[i], grad_hbm.at[i], part_give.at[i])

    def scatter(i, carry):
        row = lax.broadcasted_iota(jnp.int32, (chunk, idx.shape[1]), 0) + i * chunk
        hot = jnp.where(row == idx, 1.0, 0.0).astype(BF)
        full = spread_ref[i].astype(F32) + jnp.dot(hot, merged, preferred_element_type=F32)
        grad[i] = full.astype(BF)
        leave(i).start()
        return carry

    lax.fori_loop(0, half, scatter, 0)

    def drain(i, carry):
        leave(i).wait()
        return carry

    lax.fori_loop(0, half, drain, 0)
    for c in moves:
        c.wait()


def local(
    n_wide,
    n_narrow,
    features,
    adjacency,
    block_rows,
    block_cols,
    block_count,
    node_count,
    halo_index,
    weight,
    bias,
    out_grad,
):
    nodes, width = features.shape
    slots, side, _ = adjacency.shape
    row_blocks = nodes // side
    sides, halo = halo_index.shape[1:]
    halo_blocks = sides * halo // side
    col_blocks = row_blocks + halo_blocks
    vm = pl.BlockSpec(memory_space=pltpu.VMEM)
    sm = pl.BlockSpec(memory_space=pltpu.SMEM)
    hb = pl.BlockSpec(memory_space=ANY)
    dma = pltpu.SemaphoreType.DMA
    shape = jax.ShapeDtypeStruct
    blocked = (row_blocks, side, width)
    lanes = -(-slots // 128) * 128
    slab = width // n_wide
    part_width = width // n_narrow
    scale = 1.0 / math.sqrt(nodes * n_wide * n_narrow)
    step = 2
    chunk = 2 * side
    chunked = (nodes // chunk, chunk, width)
    half = nodes // chunk // 2
    out, own_spread, incoming, gathered, bout = pl.pallas_call(
        functools.partial(layer_kernel, n_wide, n_narrow, scale, step),
        name="layer",
        out_shape=(
            pltpu.VMEM(blocked, BF),
            pltpu.VMEM(blocked, BF),
            pltpu.VMEM((sides, halo, width), BF),
            pltpu.VMEM((n_wide, n_narrow, slab, part_width), BF),
            pltpu.VMEM((1, width), F32),
        ),
        in_specs=[vm, vm, vm, sm, sm, vm, hb, hb, hb, hb],
        out_specs=(vm,) * 5,
        scratch_shapes=[
            pltpu.VMEM((8, lanes), jnp.int32),
            pltpu.VMEM((8, lanes), jnp.int32),
            pltpu.SMEM((8, lanes), jnp.int32),
            pltpu.VMEM((col_blocks, side, width), BF),
            pltpu.VMEM((slots, side, side), BF),
            pltpu.VMEM((width, width), BF),
            pltpu.VMEM((slots, side, width), F32),
            pltpu.VMEM((sides, halo, width), BF),
            pltpu.VMEM((sides, halo, width), BF),
            pltpu.VMEM((sides, halo, width), BF),
            pltpu.VMEM((width, width), F32),
            pltpu.VMEM((n_wide, slab, width), BF),
            pltpu.VMEM((8, width), F32),
            pltpu.VMEM((1, width), F32),
            pltpu.VMEM((n_wide, slab, width), BF),
            pltpu.VMEM((n_narrow, slab, part_width), BF),
            pltpu.VMEM((n_narrow, slab, part_width), BF),
            pltpu.VMEM((n_narrow, slab, part_width), BF),
            pltpu.VMEM((n_wide, 1, width), F32),
            pltpu.VMEM((1, width), F32),
            pltpu.VMEM((n_narrow, 1, width), F32),
            dma((6,)),
        ]
        + [dma((sides,))] * 2
        + [dma((sides, halo // side))] * 2
        + [dma((n_wide,))] * 2
        + [dma((n_narrow,))] * 4
        + [dma((n_wide,))] * 4
        + [dma((n_narrow,))] * 2,
        compiler_params=pltpu.CompilerParams(
            collective_id=0, has_side_effects=True, vmem_limit_bytes=VMEM_LIMIT
        ),
    )(
        halo_index,
        block_rows,
        block_cols,
        block_count,
        node_count,
        bias.reshape(1, width),
        features.reshape(blocked),
        adjacency,
        out_grad.reshape(blocked),
        weight,
    )
    input_grad, out, wout, bout = pl.pallas_call(
        finish_kernel,
        name="finish",
        out_shape=(
            shape(chunked, BF),
            shape(blocked, BF),
            shape((width, width), F32),
            shape((1, width), F32),
        ),
        in_specs=[vm] * 6,
        out_specs=(hb, hb, hb, hb),
        scratch_shapes=[
            pltpu.VMEM((half, chunk, width), BF),
            pltpu.VMEM((width, width), F32),
            dma((4,)),
            dma((half,)),
        ],
        compiler_params=pltpu.CompilerParams(vmem_limit_bytes=FINISH_LIMIT),
    )(halo_index, own_spread.reshape(chunked), incoming, out, gathered, bout)
    return out.reshape(nodes, width), input_grad.reshape(nodes, width), wout, bout.reshape(width)


def solution(mesh):
    both = ("wide", "narrow")
    placed = (
        P(both, None),
        P(both, None, None),
        P(both, None),
        P(both, None),
        P(both),
        P(both),
        P(both, None, None),
        P(),
        P(),
        P(both, None),
    )
    return jax.shard_map(
        functools.partial(local, mesh.shape["wide"], mesh.shape["narrow"]),
        mesh=mesh,
        in_specs=placed,
        out_specs=(P(both, None), P(both, None), P(), P()),
        check_vma=False,
    )
```

```python
import functools
import math

import jax
import jax.numpy as jnp
from jax import lax
from jax.experimental import pallas as pl
from jax.experimental.pallas import tpu as pltpu
from jax.sharding import PartitionSpec as P

MESH = pl.DeviceIdType.MESH
ANY = pl.ANY
VMEM_LIMIT = 48 * 1024 * 1024
FINISH_LIMIT = 16 * 1024 * 1024
BF = jnp.bfloat16
F32 = jnp.float32


def neighbours(n_wide, n_narrow):
    w = lax.axis_index("wide")
    n = lax.axis_index("narrow")
    return (
        (w > 0, (w - 1, n)),
        (w < n_wide - 1, (w + 1, n)),
        (n > 0, (w, n - 1)),
        (n < n_narrow - 1, (w, n + 1)),
    )


def halo_copy(src, dst, send, recv, k, target):
    return pltpu.make_async_remote_copy(
        src_ref=src.at[k],
        dst_ref=dst.at[k ^ 1],
        send_sem=send.at[k],
        recv_sem=recv.at[k ^ 1],
        device_id=target,
        device_id_type=MESH,
    )


def tables(row_ref, col_ref, pads, count, row_blocks, col_blocks):
    lanes = pads.shape[1]
    slots = row_ref.shape[1]
    halo_blocks = col_blocks - row_blocks
    pads[...] = jnp.zeros(pads.shape, pads.dtype)
    pads[0:1, 0:slots] = row_ref[...]
    pads[1:2, 0:slots] = col_ref[...]
    lane = lax.broadcasted_iota(jnp.int32, (lanes, lanes), 1)
    sub = lax.broadcasted_iota(jnp.int32, (lanes, lanes), 0)
    one = lambda m: jnp.where(m, 1, 0)
    spread = lambda x: jnp.broadcast_to(x, (lanes, lanes))
    down = lambda x: jnp.sum(x, 0, keepdims=True)
    across = lambda x: jnp.sum(x, 1, keepdims=True)

    row, col = spread(pads[0:1, :]), spread(pads[1:2, :])
    row_t, col_t = jnp.transpose(row), jnp.transpose(col)
    live = lane < count
    own = live & (col < row_blocks)
    own_t = (sub < count) & (col_t < row_blocks)
    before = own_t & (sub < lane)

    def first(a, a_t):
        return own & (spread(down(one(before & (a_t == a)))) == 0)

    def order(key):
        key_t = jnp.transpose(key)
        same = (key == key_t) & (lane < sub)
        rank = across(one((key < key_t) | same))
        twin = jnp.minimum(across(one(same)), 1)
        hot = one(jnp.broadcast_to(rank, (lanes, lanes)) == lane)
        return key_t, rank, twin, lambda x: down(hot * x)

    dead = 2 * col_blocks
    lead = first(row, row_t)
    key_t, rank, twin, pick = order(
        jnp.where(lead, row, jnp.where(live, row + row_blocks, dead))
    )
    at = lane + row_blocks
    has = down(one(key_t == at))
    last = jnp.where(has > 0, down(one(key_t <= at)) - 1, lane[0:1, :])
    prev = jnp.where(twin > 0, rank - 1, row_t)
    lines = [pick(sub), pick(col_t), pick(prev), last]

    lead = first(col, col_t)
    own_key = jnp.where(lead, col + (col_blocks + 1), col + halo_blocks)
    key = jnp.where(col < row_blocks, own_key, col - row_blocks)
    unused = jnp.where(lane < slots, col_blocks, dead)
    key_t, rank, twin, pick = order(jnp.where(live, key, unused))
    has = down(one(key_t == lane))
    ends = jnp.where(has > 0, down(one(key_t <= lane)), 0)
    keep = pick(jnp.broadcast_to(twin, (lanes, lanes)))
    lines += [pick(sub), pick(row_t), keep, ends]
    slot, block = slots - 1, row_blocks - 1
    tops = (slot, col_blocks - 1, slot, slot, slot, block, 1, slots - row_blocks)
    return [jnp.clip(line, 0, top) for line, top in zip(lines, tops)]


def layer_kernel(
    n_wide,
    n_narrow,
    scale,
    step,
    idx_ref,
    row_ref,
    col_ref,
    live,
    nodes_live,
    b_ref,
    feat_hbm,
    adj_hbm,
    grad_hbm,
    w_hbm,
    grad,
    own_spread,
    incoming,
    ag_wide,
    bout_ref,
    pads,
    lined,
    table,
    ext,
    adj,
    w_ref,
    run,
    packed,
    landing,
    ret,
    wsum,
    wg,
    bsum,
    bg,
    rs_wide,
    rs_narrow,
    part,
    ag_narrow,
    b_wide,
    b_mid,
    b_narrow,
    load,
    send,
    recv,
    send_r,
    recv_r,
    send_w,
    recv_w,
    send_n,
    recv_n,
    send_gn,
    recv_gn,
    send_gw,
    recv_gw,
    send_bw,
    recv_bw,
    send_bn,
    recv_bn,
):
    w = lax.axis_index("wide")
    n = lax.axis_index("narrow")
    slots = adj.shape[0]
    row_blocks, side, width = feat_hbm.shape
    col_blocks = ext.shape[0]
    halo_blocks = col_blocks - row_blocks
    half = row_blocks // 2
    count = idx_ref.shape[2]
    per = count // side
    slab, across = rs_wide.shape[2:]
    part_width = rs_narrow.shape[3]
    keep_to = nodes_live[0]

    loads = [
        pltpu.make_async_copy(feat_hbm.at[pl.ds(0, half)], ext.at[pl.ds(0, half)], load.at[0]),
        pltpu.make_async_copy(feat_hbm.at[pl.ds(half, half)], ext.at[pl.ds(half, half)], load.at[1]),
        pltpu.make_async_copy(adj_hbm, adj, load.at[2]),
        pltpu.make_async_copy(w_hbm, w_ref, load.at[3]),
        pltpu.make_async_copy(grad_hbm, grad, load.at[4]),
    ]
    for fetch in loads:
        fetch.start()

    def wide_peer(d):
        return (lax.rem(w + d, n_wide), n)

    def narrow_peer(d):
        return (w, lax.rem(n + d, n_narrow))

    def remote(src, dst, s, r, peer):
        return pltpu.make_async_remote_copy(
            src_ref=src, dst_ref=dst, send_sem=s, recv_sem=r, device_id=peer, device_id_type=MESH
        )

    near = neighbours(n_wide, n_narrow)
    peers = [wide_peer(d) for d in range(1, n_wide)] + [
        narrow_peer(d) for d in range(1, n_narrow)
    ]
    barrier = pltpu.get_barrier_semaphore()
    for peer in peers:
        pl.semaphore_signal(barrier, inc=1, device_id=peer, device_id_type=MESH)

    for i, line in enumerate(tables(row_ref, col_ref, pads, live[0], row_blocks, col_blocks)):
        lined[pl.ds(i, 1), :] = line
    tabled = pltpu.make_async_copy(lined, table, load.at[5])
    tabled.start()

    ext[pl.ds(row_blocks, halo_blocks)] = jnp.zeros((halo_blocks, side, width), BF)
    wsum[...] = jnp.zeros_like(wsum)
    bsum[...] = jnp.zeros_like(bsum)
    loads[0].wait()
    span = half * side
    lane = lax.broadcasted_iota(jnp.int32, (count, 128), 1).astype(F32)

    def pack(k):
        row = idx_ref[0, pl.ds(k, 1), :].astype(F32)
        column = jnp.transpose(jnp.broadcast_to(row, (128, count)))
        hot = jnp.concatenate(
            [jnp.where(column == lane + float(at), 1.0, 0.0).astype(BF) for at in range(0, span, 128)],
            axis=1,
        )
        near_rows = ext[pl.ds(0, half)].reshape(span, width)
        packed[k] = jnp.dot(hot, near_rows, preferred_element_type=F32).astype(BF)

    pack(2)
    pl.semaphore_wait(barrier, len(peers))
    for k in (2, 3, 1, 0):
        there, target = near[k]
        if k != 2:
            pack(k)

        @pl.when(there)
        def _():
            halo_copy(packed, landing, send, recv, k, target).start()

    def kept(block, blocks=1):
        at = lax.broadcasted_iota(jnp.int32, (blocks * side, width), 0)
        return at < keep_to - block * side

    loads[1].wait()

    def mask(i, carry):
        ext[i] = jnp.where(kept(i), ext[i].astype(F32), 0.0).astype(BF)
        return carry

    lax.fori_loop(half, row_blocks, mask, 0)
    loads[2].wait()
    tabled.wait()

    def product(k):
        return jnp.dot(adj[table[0, k]], ext[table[1, k]], preferred_element_type=F32)

    unroll = 16

    def leading(t, carry):
        for u in range(unroll):
            k = t * unroll + u
            run[k] = product(k)
        return carry

    lax.fori_loop(0, row_blocks // unroll, leading, 0)
    for k in (1, 0, 2, 3):
        there, target = near[k]

        @pl.when(there)
        def _():
            halo_copy(packed, landing, send, recv, k, target).wait_send()
            halo_copy(packed, landing, send, recv, k ^ 1, target).wait_recv()
            ext[pl.ds(row_blocks + k * per, per)] = landing[k].reshape(per, side, width)

    def following(t, carry):
        for u in range(unroll):
            k = t * unroll + u
            run[k] = run[table[2, k]] + product(k)
        return carry

    lax.fori_loop(row_blocks // unroll, slots // unroll, following, 0)
    loads[3].wait()
    loads[4].wait()

    tall = step * side

    def into(i, h):
        at = pl.ds(i * step, step)
        if h == 0:
            agg = jnp.concatenate([run[table[3, i * step + j]] for j in range(step)], 0).astype(BF)
            own_spread[at] = agg.reshape(step, side, width)
        else:
            agg = own_spread[at].reshape(tall, width)
        return agg, jnp.dot(agg, w_ref[:, cut(h)], preferred_element_type=F32)

    def cut(h):
        return slice(h * across, (h + 1) * across)

    def middle(i, pre, h):
        at = pl.ds(i * step, step)
        g = grad[at, :, cut(h)].reshape(tall, across).astype(F32)
        pre = pre + b_ref[:, cut(h)]
        at_row = lax.broadcasted_iota(jnp.int32, (tall, across), 0)
        keep = at_row < keep_to - i * tall
        sig = 0.5 * jnp.tanh(0.5 * pre) + 0.5
        act = pre * sig
        grad[at, :, cut(h)] = jnp.where(keep, act, 0.0).astype(BF).reshape(step, side, across)
        dpre = jnp.where(keep, g * (sig + act * (1.0 - sig)), 0.0).astype(BF)
        bsum[:, cut(h)] += jnp.sum(dpre.astype(F32).reshape(tall // 8, 8, across), 0)
        return dpre

    def after(i, agg, dpre, h):
        wsum[h] += lax.dot_general(
            agg, dpre, (((0,), (0,)), ((), ())), preferred_element_type=F32
        )
        ext[pl.ds(i * step, step), :, cut(h)] = dpre.reshape(step, side, across)

    group = row_blocks // step // 2

    def dense(h):
        def body(t, carry):
            now = into(t * group, h)
            for u in range(group):
                i = t * group + u
                later = into(i + 1, h) if u + 1 < group else None
                dpre = middle(i, now[1], h)
                after(i, now[0], dpre, h)
                now = later
            return carry

        lax.fori_loop(0, row_blocks // step // group, body, 0)

    def scatter_wide(h):
        wg[h] = wsum[h].astype(BF).reshape(n_wide, slab, across)
        copies = []
        for d in range(1, n_wide):
            peer = wide_peer(d)
            c = remote(
                wg.at[h, peer[0]], rs_wide.at[h, d], send_w.at[h, d], recv_w.at[h, d], peer
            )
            c.start()
            copies.append(c)
        return copies

    def scatter_narrow(h, arrived):
        total = wg[h, w].astype(F32)
        for c in arrived:
            c.wait_recv()
        for d in range(1, n_wide):
            total = total + rs_wide[h, d].astype(F32)
        for j in range(n_narrow):
            part[h, j] = total[:, j * part_width : (j + 1) * part_width].astype(BF)
        copies = []
        for d in range(1, n_narrow):
            peer = narrow_peer(d)
            c = remote(
                part.at[h, peer[1]], rs_narrow.at[h, d], send_n.at[h, d], recv_n.at[h, d], peer
            )
            c.start()
            copies.append(c)
        return copies

    def share_narrow(h, arrived):
        piece = part[h, n].astype(F32)
        for c in arrived:
            c.wait_recv()
        for d in range(1, n_narrow):
            piece = piece + rs_narrow[h, d].astype(F32)
        ag_narrow[h, n] = (piece * scale).astype(BF)
        copies = []
        for d in range(1, n_narrow):
            mine = ag_narrow.at[h, n]
            c = remote(mine, mine, send_gn.at[h, d], recv_gn.at[h, d], narrow_peer(d))
            c.start()
            copies.append(c)
        return copies

    def share_wide(h, arrived):
        for c in arrived:
            c.wait_recv()
        copies = []
        for d in range(1, n_wide):
            c = remote(
                ag_narrow.at[h], ag_wide.at[h, w], send_gw.at[h, d], recv_gw.at[h, d], wide_peer(d)
            )
            c.start()
            copies.append(c)
        ag_wide[h, w] = ag_narrow[h]
        return copies

    dense(0)
    first = [scatter_wide(0)]
    dense(1)
    first.append(scatter_wide(1))
    bg[...] = jnp.sum(bsum[...], 0, keepdims=True)
    bias_first = []
    for d in range(1, n_wide):
        c = remote(bg, b_wide.at[d], send_bw.at[d], recv_bw.at[d], wide_peer(d))
        c.start()
        bias_first.append(c)
    second = [scatter_narrow(0, first[0])]
    run[0] = jnp.zeros(run.shape[1:], run.dtype)
    deep = 8

    def backed(t, carry):
        at = pl.ds(t * deep, deep)
        ext[at] = (
            lax.dot_general(
                ext[at].reshape(deep * side, width),
                w_ref[...],
                (((1,), (1,)), ((), ())),
                preferred_element_type=F32,
            )
            .astype(BF)
            .reshape(deep, side, width)
        )
        return carry

    lax.fori_loop(0, row_blocks // deep, backed, 0)
    third = [share_narrow(0, second[0])]

    def spreading(k):
        return lax.dot_general(
            adj[table[4, k]], ext[table[5, k]], (((0,), (0,)), ((), ())), preferred_element_type=F32
        )

    def backward(t, carry):
        held = run[t * unroll]
        for u in range(unroll):
            k = t * unroll + u
            held = held * table[6, k].astype(F32) + spreading(k)
            run[k + 1] = held
        return carry

    early = slots - row_blocks
    lax.fori_loop(0, early // unroll, backward, 0)
    fourth = [share_wide(0, third[0])]
    second.append(scatter_narrow(1, first[1]))
    bias = bg[...]
    for c in bias_first:
        c.wait_recv()
    for d in range(1, n_wide):
        bias = bias + b_wide[d]
    b_mid[...] = bias
    bias_second = []
    for d in range(1, n_narrow):
        c = remote(b_mid, b_narrow.at[d], send_bn.at[d], recv_bn.at[d], narrow_peer(d))
        c.start()
        bias_second.append(c)

    def returned(k, j):
        at = pl.ds(j * side, side)
        return pltpu.make_async_remote_copy(
            src_ref=ret.at[k, at],
            dst_ref=incoming.at[k ^ 1, at],
            send_sem=send_r.at[k, j],
            recv_sem=recv_r.at[k ^ 1, j],
            device_id=near[k][1],
            device_id_type=MESH,
        )

    def give_back(k, j):
        ret[k, pl.ds(j * side, side), :] = run[table[7, k * per + j]].astype(BF)

        @pl.when(near[k][0])
        def _():
            returned(k, j).start()

        @pl.when(jnp.logical_not(near[k][0]))
        def _():
            incoming[k, pl.ds(j * side, side), :] = jnp.zeros((side, width), BF)

    early_return = [(k, j) for k in (2, 3) for j in range(per // 2)]
    early_return += [(k, j) for k in (1, 0) for j in range(per)]
    for k, j in early_return:
        give_back(k, j)

    def own(c):
        return run[table[7, halo_blocks + c]] + spreading(early + c)

    def low(t, carry):
        for u in range(unroll):
            c = t * unroll + u
            own_spread[c] = own(c).astype(BF)
        return carry

    lax.fori_loop(0, half // unroll, low, 0)
    third.append(share_narrow(1, second[1]))
    for c in bias_second:
        c.wait_recv()
    for d in range(1, n_narrow):
        bias = bias + b_narrow[d]
    bout_ref[...] = bias * scale
    for k in (2, 3):
        for j in range(per // 2, per):
            give_back(k, j)

    def high(t, carry):
        for u in range(unroll):
            c = t * unroll + u
            own_spread[c] = jnp.where(kept(c), own(c), 0.0).astype(BF)
        return carry

    lax.fori_loop(half // unroll, row_blocks // unroll, high, 0)
    fourth.append(share_wide(1, third[1]))
    for k in range(4):
        there, target = near[k]

        @pl.when(there)
        def _():
            for j in range(per):
                returned(k, j).wait_send()
                returned(k ^ 1, j).wait_recv()

    for copies in fourth:
        for c in copies:
            c.wait_recv()
    for copies in first + second + third + fourth + [bias_first, bias_second]:
        for c in copies:
            c.wait_send()


def finish_kernel(
    idx_ref,
    spread_ref,
    incoming,
    out_ref,
    ag_wide,
    b_ref,
    grad_hbm,
    out_hbm,
    w_hbm,
    b_hbm,
    grad,
    wg,
    give,
    part_give,
):
    half, chunk, width = grad.shape
    parts, n_wide, n_narrow, slab, part_width = ag_wide.shape
    moves = [
        pltpu.make_async_copy(out_ref, out_hbm, give.at[0]),
        pltpu.make_async_copy(
            spread_ref.at[pl.ds(half, half)], grad_hbm.at[pl.ds(half, half)], give.at[1]
        ),
        pltpu.make_async_copy(b_ref, b_hbm, give.at[2]),
    ]
    for c in moves:
        c.start()
    for i in range(n_wide):
        line = [ag_wide[h, i, j] for h in range(parts) for j in range(n_narrow)]
        wg[pl.ds(i * slab, slab), :] = jnp.concatenate(line, 1).astype(F32)
    moves.append(pltpu.make_async_copy(wg, w_hbm, give.at[3]))
    moves[3].start()
    merged = incoming[...].reshape(-1, width)
    idx = jnp.concatenate([idx_ref[0, k : k + 1, :] for k in range(incoming.shape[0])], 1)

    def leave(i):
        return pltpu.make_async_copy(grad.at[i], grad_hbm.at[i], part_give.at[i])

    def scatter(i, carry):
        row = lax.broadcasted_iota(jnp.int32, (chunk, idx.shape[1]), 0) + i * chunk
        hot = jnp.where(row == idx, 1.0, 0.0).astype(BF)
        full = spread_ref[i].astype(F32) + jnp.dot(hot, merged, preferred_element_type=F32)
        grad[i] = full.astype(BF)
        leave(i).start()
        return carry

    lax.fori_loop(0, half, scatter, 0)

    def drain(i, carry):
        leave(i).wait()
        return carry

    lax.fori_loop(0, half, drain, 0)
    for c in moves:
        c.wait()


def local(
    n_wide,
    n_narrow,
    features,
    adjacency,
    block_rows,
    block_cols,
    block_count,
    node_count,
    halo_index,
    weight,
    bias,
    out_grad,
):
    nodes, width = features.shape
    slots, side, _ = adjacency.shape
    row_blocks = nodes // side
    sides, halo = halo_index.shape[1:]
    halo_blocks = sides * halo // side
    col_blocks = row_blocks + halo_blocks
    vm = pl.BlockSpec(memory_space=pltpu.VMEM)
    sm = pl.BlockSpec(memory_space=pltpu.SMEM)
    hb = pl.BlockSpec(memory_space=ANY)
    dma = pltpu.SemaphoreType.DMA
    shape = jax.ShapeDtypeStruct
    blocked = (row_blocks, side, width)
    lanes = -(-slots // 128) * 128
    slab = width // n_wide
    parts = 2
    across = width // parts
    part_width = across // n_narrow
    scale = 1.0 / math.sqrt(nodes * n_wide * n_narrow)
    step = 4
    chunk = 2 * side
    chunked = (nodes // chunk, chunk, width)
    half = nodes // chunk // 2
    out, own_spread, incoming, gathered, bout = pl.pallas_call(
        functools.partial(layer_kernel, n_wide, n_narrow, scale, step),
        name="layer",
        out_shape=(
            pltpu.VMEM(blocked, BF),
            pltpu.VMEM(blocked, BF),
            pltpu.VMEM((sides, halo, width), BF),
            pltpu.VMEM((parts, n_wide, n_narrow, slab, part_width), BF),
            pltpu.VMEM((1, width), F32),
        ),
        in_specs=[vm, vm, vm, sm, sm, vm, hb, hb, hb, hb],
        out_specs=(vm,) * 5,
        scratch_shapes=[
            pltpu.VMEM((8, lanes), jnp.int32),
            pltpu.VMEM((8, lanes), jnp.int32),
            pltpu.SMEM((8, lanes), jnp.int32),
            pltpu.VMEM((col_blocks, side, width), BF),
            pltpu.VMEM((slots, side, side), BF),
            pltpu.VMEM((width, width), BF),
            pltpu.VMEM((slots, side, width), F32),
            pltpu.VMEM((sides, halo, width), BF),
            pltpu.VMEM((sides, halo, width), BF),
            pltpu.VMEM((sides, halo, width), BF),
            pltpu.VMEM((parts, width, across), F32),
            pltpu.VMEM((parts, n_wide, slab, across), BF),
            pltpu.VMEM((8, width), F32),
            pltpu.VMEM((1, width), F32),
            pltpu.VMEM((parts, n_wide, slab, across), BF),
            pltpu.VMEM((parts, n_narrow, slab, part_width), BF),
            pltpu.VMEM((parts, n_narrow, slab, part_width), BF),
            pltpu.VMEM((parts, n_narrow, slab, part_width), BF),
            pltpu.VMEM((n_wide, 1, width), F32),
            pltpu.VMEM((1, width), F32),
            pltpu.VMEM((n_narrow, 1, width), F32),
            dma((6,)),
        ]
        + [dma((sides,))] * 2
        + [dma((sides, halo // side))] * 2
        + [dma((parts, n_wide))] * 2
        + [dma((parts, n_narrow))] * 4
        + [dma((parts, n_wide))] * 2
        + [dma((n_wide,))] * 2
        + [dma((n_narrow,))] * 2,
        compiler_params=pltpu.CompilerParams(
            collective_id=0, has_side_effects=True, vmem_limit_bytes=VMEM_LIMIT
        ),
    )(
        halo_index,
        block_rows,
        block_cols,
        block_count,
        node_count,
        bias.reshape(1, width),
        features.reshape(blocked),
        adjacency,
        out_grad.reshape(blocked),
        weight,
    )
    input_grad, out, wout, bout = pl.pallas_call(
        finish_kernel,
        name="finish",
        out_shape=(
            shape(chunked, BF),
            shape(blocked, BF),
            shape((width, width), F32),
            shape((1, width), F32),
        ),
        in_specs=[vm] * 6,
        out_specs=(hb, hb, hb, hb),
        scratch_shapes=[
            pltpu.VMEM((half, chunk, width), BF),
            pltpu.VMEM((width, width), F32),
            dma((4,)),
            dma((half,)),
        ],
        compiler_params=pltpu.CompilerParams(vmem_limit_bytes=FINISH_LIMIT),
    )(halo_index, own_spread.reshape(chunked), incoming, out, gathered, bout)
    return out.reshape(nodes, width), input_grad.reshape(nodes, width), wout, bout.reshape(width)


def solution(mesh):
    both = ("wide", "narrow")
    placed = (
        P(both, None),
        P(both, None, None),
        P(both, None),
        P(both, None),
        P(both),
        P(both),
        P(both, None, None),
        P(),
        P(),
        P(both, None),
    )
    return jax.shard_map(
        functools.partial(local, mesh.shape["wide"], mesh.shape["narrow"]),
        mesh=mesh,
        in_specs=placed,
        out_specs=(P(both, None), P(both, None), P(), P()),
        check_vma=False,
    )
```

```python
import functools
import math

import jax
import jax.numpy as jnp
from jax import lax
from jax.experimental import pallas as pl
from jax.experimental.pallas import tpu as pltpu
from jax.sharding import PartitionSpec as P

MESH = pl.DeviceIdType.MESH
ANY = pl.ANY
VMEM_LIMIT = 48 * 1024 * 1024
FINISH_LIMIT = 16 * 1024 * 1024
BF = jnp.bfloat16
F32 = jnp.float32


def neighbours(n_wide, n_narrow):
    w = lax.axis_index("wide")
    n = lax.axis_index("narrow")
    return (
        (w > 0, (w - 1, n)),
        (w < n_wide - 1, (w + 1, n)),
        (n > 0, (w, n - 1)),
        (n < n_narrow - 1, (w, n + 1)),
    )


def halo_copy(src, dst, send, recv, k, target):
    return pltpu.make_async_remote_copy(
        src_ref=src.at[k],
        dst_ref=dst.at[k ^ 1],
        send_sem=send.at[k],
        recv_sem=recv.at[k ^ 1],
        device_id=target,
        device_id_type=MESH,
    )


def tables(row_ref, col_ref, pads, count, row_blocks, col_blocks):
    lanes = pads.shape[1]
    slots = row_ref.shape[1]
    halo_blocks = col_blocks - row_blocks
    pads[...] = jnp.zeros(pads.shape, pads.dtype)
    pads[0:1, 0:slots] = row_ref[...]
    pads[1:2, 0:slots] = col_ref[...]
    lane = lax.broadcasted_iota(jnp.int32, (lanes, lanes), 1)
    sub = lax.broadcasted_iota(jnp.int32, (lanes, lanes), 0)
    one = lambda m: jnp.where(m, 1, 0)
    spread = lambda x: jnp.broadcast_to(x, (lanes, lanes))
    down = lambda x: jnp.sum(x, 0, keepdims=True)
    across = lambda x: jnp.sum(x, 1, keepdims=True)

    row, col = spread(pads[0:1, :]), spread(pads[1:2, :])
    row_t, col_t = jnp.transpose(row), jnp.transpose(col)
    live = lane < count
    own = live & (col < row_blocks)
    own_t = (sub < count) & (col_t < row_blocks)
    before = own_t & (sub < lane)

    def first(a, a_t):
        return own & (spread(down(one(before & (a_t == a)))) == 0)

    def order(key):
        key_t = jnp.transpose(key)
        same = (key == key_t) & (lane < sub)
        rank = across(one((key < key_t) | same))
        twin = jnp.minimum(across(one(same)), 1)
        hot = one(jnp.broadcast_to(rank, (lanes, lanes)) == lane)
        return key_t, rank, twin, lambda x: down(hot * x)

    dead = 2 * col_blocks
    lead = first(row, row_t)
    key_t, rank, twin, pick = order(
        jnp.where(lead, row, jnp.where(live, row + row_blocks, dead))
    )
    at = lane + row_blocks
    has = down(one(key_t == at))
    last = jnp.where(has > 0, down(one(key_t <= at)) - 1, lane[0:1, :])
    prev = jnp.where(twin > 0, rank - 1, row_t)
    lines = [pick(sub), pick(col_t), pick(prev), last]

    lead = first(col, col_t)
    own_key = jnp.where(lead, col + (col_blocks + 1), col + halo_blocks)
    key = jnp.where(col < row_blocks, own_key, col - row_blocks)
    unused = jnp.where(lane < slots, col_blocks, dead)
    key_t, rank, twin, pick = order(jnp.where(live, key, unused))
    has = down(one(key_t == lane))
    ends = jnp.where(has > 0, down(one(key_t <= lane)), 0)
    keep = pick(jnp.broadcast_to(twin, (lanes, lanes)))
    lines += [pick(sub), pick(row_t), keep, ends]
    slot, block = slots - 1, row_blocks - 1
    tops = (slot, col_blocks - 1, slot, slot, slot, block, 1, slots - row_blocks)
    return [jnp.clip(line, 0, top) for line, top in zip(lines, tops)]


def layer_kernel(
    n_wide,
    n_narrow,
    scale,
    step,
    idx_ref,
    row_ref,
    col_ref,
    live,
    nodes_live,
    b_ref,
    feat_hbm,
    adj_hbm,
    grad_hbm,
    w_hbm,
    grad,
    own_spread,
    incoming,
    ag_wide,
    bout_ref,
    pads,
    lined,
    table,
    ext,
    adj,
    w_ref,
    run,
    packed,
    landing,
    ret,
    wsum,
    wg,
    bsum,
    bg,
    rs_wide,
    rs_narrow,
    part,
    ag_narrow,
    b_wide,
    b_mid,
    b_narrow,
    load,
    send,
    recv,
    send_r,
    recv_r,
    send_w,
    recv_w,
    send_n,
    recv_n,
    send_gn,
    recv_gn,
    send_gw,
    recv_gw,
    send_bw,
    recv_bw,
    send_bn,
    recv_bn,
):
    w = lax.axis_index("wide")
    n = lax.axis_index("narrow")
    slots = adj.shape[0]
    row_blocks, side, width = feat_hbm.shape
    col_blocks = ext.shape[0]
    halo_blocks = col_blocks - row_blocks
    half = row_blocks // 2
    count = idx_ref.shape[2]
    per = count // side
    slab, across = rs_wide.shape[2:]
    lines = rs_narrow.shape[2]
    keep_to = nodes_live[0]

    loads = [
        pltpu.make_async_copy(feat_hbm.at[pl.ds(0, half)], ext.at[pl.ds(0, half)], load.at[0]),
        pltpu.make_async_copy(feat_hbm.at[pl.ds(half, half)], ext.at[pl.ds(half, half)], load.at[1]),
        pltpu.make_async_copy(adj_hbm, adj, load.at[2]),
        pltpu.make_async_copy(w_hbm, w_ref, load.at[3]),
        pltpu.make_async_copy(grad_hbm, grad, load.at[4]),
    ]
    loads[0].start()

    def wide_peer(d):
        return (lax.rem(w + d, n_wide), n)

    def narrow_peer(d):
        return (w, lax.rem(n + d, n_narrow))

    def remote(src, dst, s, r, peer):
        return pltpu.make_async_remote_copy(
            src_ref=src, dst_ref=dst, send_sem=s, recv_sem=r, device_id=peer, device_id_type=MESH
        )

    near = neighbours(n_wide, n_narrow)
    peers = [wide_peer(d) for d in range(1, n_wide)] + [
        narrow_peer(d) for d in range(1, n_narrow)
    ]
    barrier = pltpu.get_barrier_semaphore()
    for peer in peers:
        pl.semaphore_signal(barrier, inc=1, device_id=peer, device_id_type=MESH)

    for i, line in enumerate(tables(row_ref, col_ref, pads, live[0], row_blocks, col_blocks)):
        lined[pl.ds(i, 1), :] = line
    tabled = pltpu.make_async_copy(lined, table, load.at[5])
    tabled.start()

    ext[pl.ds(row_blocks, halo_blocks)] = jnp.zeros((halo_blocks, side, width), BF)
    wsum[...] = jnp.zeros_like(wsum)
    bsum[...] = jnp.zeros_like(bsum)
    loads[0].wait()
    for fetch in loads[1:3]:
        fetch.start()
    span = half * side
    lane = lax.broadcasted_iota(jnp.int32, (count, 128), 1).astype(F32)

    def pack(k):
        row = idx_ref[0, pl.ds(k, 1), :].astype(F32)
        column = jnp.transpose(jnp.broadcast_to(row, (128, count)))
        hot = jnp.concatenate(
            [jnp.where(column == lane + float(at), 1.0, 0.0).astype(BF) for at in range(0, span, 128)],
            axis=1,
        )
        near_rows = ext[pl.ds(0, half)].reshape(span, width)
        packed[k] = jnp.dot(hot, near_rows, preferred_element_type=F32).astype(BF)

    pack(2)
    pl.semaphore_wait(barrier, len(peers))
    for k in (2, 3, 1, 0):
        there, target = near[k]
        if k != 2:
            pack(k)

        @pl.when(there)
        def _():
            halo_copy(packed, landing, send, recv, k, target).start()

    for fetch in loads[3:]:
        fetch.start()

    def kept(block, blocks=1):
        at = lax.broadcasted_iota(jnp.int32, (blocks * side, width), 0)
        return at < keep_to - block * side

    loads[1].wait()

    def mask(i, carry):
        ext[i] = jnp.where(kept(i), ext[i].astype(F32), 0.0).astype(BF)
        return carry

    lax.fori_loop(half, row_blocks, mask, 0)
    loads[2].wait()
    tabled.wait()

    def product(k):
        return jnp.dot(adj[table[0, k]], ext[table[1, k]], preferred_element_type=F32)

    unroll = 16

    def leading(t, carry):
        for u in range(unroll):
            k = t * unroll + u
            run[k] = product(k)
        return carry

    lax.fori_loop(0, row_blocks // unroll, leading, 0)
    for k in (1, 0, 2, 3):
        there, target = near[k]

        @pl.when(there)
        def _():
            halo_copy(packed, landing, send, recv, k, target).wait_send()
            halo_copy(packed, landing, send, recv, k ^ 1, target).wait_recv()
            ext[pl.ds(row_blocks + k * per, per)] = landing[k].reshape(per, side, width)

    def following(t, carry):
        for u in range(unroll):
            k = t * unroll + u
            run[k] = run[table[2, k]] + product(k)
        return carry

    lax.fori_loop(row_blocks // unroll, slots // unroll, following, 0)
    loads[3].wait()
    loads[4].wait()

    tall = step * side

    def into(i, h):
        at = pl.ds(i * step, step)
        if h == 0:
            agg = jnp.concatenate([run[table[3, i * step + j]] for j in range(step)], 0).astype(BF)
            own_spread[at] = agg.reshape(step, side, width)
        else:
            agg = own_spread[at].reshape(tall, width)
        return agg, jnp.dot(agg, w_ref[:, cut(h)], preferred_element_type=F32)

    def cut(h):
        return slice(h * across, (h + 1) * across)

    def middle(i, pre, h):
        at = pl.ds(i * step, step)
        g = grad[at, :, cut(h)].reshape(tall, across).astype(F32)
        pre = pre + b_ref[:, cut(h)]
        at_row = lax.broadcasted_iota(jnp.int32, (tall, across), 0)
        keep = at_row < keep_to - i * tall
        sig = 0.5 * jnp.tanh(0.5 * pre) + 0.5
        act = pre * sig
        grad[at, :, cut(h)] = jnp.where(keep, act, 0.0).astype(BF).reshape(step, side, across)
        dpre = jnp.where(keep, g * (sig + act * (1.0 - sig)), 0.0).astype(BF)
        bsum[:, cut(h)] += jnp.sum(dpre.astype(F32).reshape(tall // 8, 8, across), 0)
        return dpre

    def after(i, agg, dpre, h):
        wsum[h] += lax.dot_general(
            agg, dpre, (((0,), (0,)), ((), ())), preferred_element_type=F32
        )
        ext[pl.ds(i * step, step), :, cut(h)] = dpre.reshape(step, side, across)

    group = row_blocks // step // 2

    def dense(h):
        def body(t, carry):
            now = into(t * group, h)
            for u in range(group):
                i = t * group + u
                later = into(i + 1, h) if u + 1 < group else None
                dpre = middle(i, now[1], h)
                after(i, now[0], dpre, h)
                now = later
            return carry

        lax.fori_loop(0, row_blocks // step // group, body, 0)

    def scatter_wide(h):
        wg[h] = wsum[h].astype(BF).reshape(n_wide, slab, across)
        copies = []
        for d in range(1, n_wide):
            peer = wide_peer(d)
            c = remote(
                wg.at[h, peer[0]], rs_wide.at[h, d], send_w.at[h, d], recv_w.at[h, d], peer
            )
            c.start()
            copies.append(c)
        return copies

    def scatter_narrow(h, arrived):
        total = wg[h, w].astype(F32)
        for c in arrived:
            c.wait_recv()
        for d in range(1, n_wide):
            total = total + rs_wide[h, d].astype(F32)
        for j in range(n_narrow):
            part[h, j] = total[j * lines : (j + 1) * lines].astype(BF)
        copies = []
        for d in range(1, n_narrow):
            peer = narrow_peer(d)
            c = remote(
                part.at[h, peer[1]], rs_narrow.at[h, d], send_n.at[h, d], recv_n.at[h, d], peer
            )
            c.start()
            copies.append(c)
        return copies

    def share_narrow(h, arrived):
        piece = part[h, n].astype(F32)
        for c in arrived:
            c.wait_recv()
        for d in range(1, n_narrow):
            piece = piece + rs_narrow[h, d].astype(F32)
        ag_narrow[h, n] = (piece * scale).astype(BF)
        copies = []
        for d in range(1, n_narrow):
            mine = ag_narrow.at[h, n]
            c = remote(mine, mine, send_gn.at[h, d], recv_gn.at[h, d], narrow_peer(d))
            c.start()
            copies.append(c)
        return copies

    def share_wide(h, arrived):
        for c in arrived:
            c.wait_recv()
        copies = []
        for d in range(1, n_wide):
            c = remote(
                ag_narrow.at[h], ag_wide.at[h, w], send_gw.at[h, d], recv_gw.at[h, d], wide_peer(d)
            )
            c.start()
            copies.append(c)
        ag_wide[h, w] = ag_narrow[h]
        return copies

    dense(0)
    first = [scatter_wide(0)]
    dense(1)
    first.append(scatter_wide(1))
    bg[...] = jnp.sum(bsum[...], 0, keepdims=True)
    bias_first = []
    for d in range(1, n_wide):
        c = remote(bg, b_wide.at[d], send_bw.at[d], recv_bw.at[d], wide_peer(d))
        c.start()
        bias_first.append(c)
    second = [scatter_narrow(0, first[0])]
    run[0] = jnp.zeros(run.shape[1:], run.dtype)
    deep = 8

    def backed(t, carry):
        at = pl.ds(t * deep, deep)
        ext[at] = (
            lax.dot_general(
                ext[at].reshape(deep * side, width),
                w_ref[...],
                (((1,), (1,)), ((), ())),
                preferred_element_type=F32,
            )
            .astype(BF)
            .reshape(deep, side, width)
        )
        return carry

    lax.fori_loop(0, row_blocks // deep, backed, 0)
    third = [share_narrow(0, second[0])]

    def spreading(k):
        return lax.dot_general(
            adj[table[4, k]], ext[table[5, k]], (((0,), (0,)), ((), ())), preferred_element_type=F32
        )

    def backward(t, carry):
        held = run[t * unroll]
        for u in range(unroll):
            k = t * unroll + u
            held = held * table[6, k].astype(F32) + spreading(k)
            run[k + 1] = held
        return carry

    early = slots - row_blocks
    lax.fori_loop(0, early // unroll, backward, 0)
    fourth = [share_wide(0, third[0])]
    second.append(scatter_narrow(1, first[1]))
    bias = bg[...]
    for c in bias_first:
        c.wait_recv()
    for d in range(1, n_wide):
        bias = bias + b_wide[d]
    b_mid[...] = bias
    bias_second = []
    for d in range(1, n_narrow):
        c = remote(b_mid, b_narrow.at[d], send_bn.at[d], recv_bn.at[d], narrow_peer(d))
        c.start()
        bias_second.append(c)

    def returned(k, j):
        at = pl.ds(j * side, side)
        return pltpu.make_async_remote_copy(
            src_ref=ret.at[k, at],
            dst_ref=incoming.at[k ^ 1, at],
            send_sem=send_r.at[k, j],
            recv_sem=recv_r.at[k ^ 1, j],
            device_id=near[k][1],
            device_id_type=MESH,
        )

    def give_back(k, j):
        ret[k, pl.ds(j * side, side), :] = run[table[7, k * per + j]].astype(BF)

        @pl.when(near[k][0])
        def _():
            returned(k, j).start()

        @pl.when(jnp.logical_not(near[k][0]))
        def _():
            incoming[k, pl.ds(j * side, side), :] = jnp.zeros((side, width), BF)

    early_return = [(k, j) for k in (2, 3) for j in range(per // 2)]
    early_return += [(k, j) for k in (1, 0) for j in range(per)]
    for k, j in early_return:
        give_back(k, j)

    def own(c):
        return run[table[7, halo_blocks + c]] + spreading(early + c)

    def low(t, carry):
        for u in range(unroll):
            c = t * unroll + u
            own_spread[c] = own(c).astype(BF)
        return carry

    lax.fori_loop(0, half // unroll, low, 0)
    third.append(share_narrow(1, second[1]))
    for c in bias_second:
        c.wait_recv()
    for d in range(1, n_narrow):
        bias = bias + b_narrow[d]
    bout_ref[...] = bias * scale
    for k in (2, 3):
        for j in range(per // 2, per):
            give_back(k, j)

    def high(t, carry):
        for u in range(unroll):
            c = t * unroll + u
            own_spread[c] = jnp.where(kept(c), own(c), 0.0).astype(BF)
        return carry

    lax.fori_loop(half // unroll, row_blocks // unroll, high, 0)
    fourth.append(share_wide(1, third[1]))
    for k in range(4):
        there, target = near[k]

        @pl.when(there)
        def _():
            for j in range(per):
                returned(k, j).wait_send()
                returned(k ^ 1, j).wait_recv()

    for copies in fourth:
        for c in copies:
            c.wait_recv()
    for copies in first + second + third + fourth + [bias_first, bias_second]:
        for c in copies:
            c.wait_send()


def finish_kernel(
    idx_ref,
    spread_ref,
    incoming,
    out_ref,
    ag_wide,
    b_ref,
    grad_hbm,
    out_hbm,
    w_hbm,
    b_hbm,
    grad,
    wg,
    give,
    part_give,
):
    half, chunk, width = grad.shape
    parts, n_wide, n_narrow, lines, across = ag_wide.shape
    moves = [
        pltpu.make_async_copy(out_ref, out_hbm, give.at[0]),
        pltpu.make_async_copy(
            spread_ref.at[pl.ds(half, half)], grad_hbm.at[pl.ds(half, half)], give.at[1]
        ),
        pltpu.make_async_copy(b_ref, b_hbm, give.at[2]),
    ]
    for c in moves:
        c.start()
    for h in range(parts):
        for i in range(n_wide):
            for j in range(n_narrow):
                at = pl.ds((i * n_narrow + j) * lines, lines)
                wg[at, h * across : (h + 1) * across] = ag_wide[h, i, j].astype(F32)
    moves.append(pltpu.make_async_copy(wg, w_hbm, give.at[3]))
    moves[3].start()
    merged = incoming[...].reshape(-1, width)
    idx = jnp.concatenate([idx_ref[0, k : k + 1, :] for k in range(incoming.shape[0])], 1)

    def leave(i):
        return pltpu.make_async_copy(grad.at[i], grad_hbm.at[i], part_give.at[i])

    def scatter(i, carry):
        row = lax.broadcasted_iota(jnp.int32, (chunk, idx.shape[1]), 0) + i * chunk
        hot = jnp.where(row == idx, 1.0, 0.0).astype(BF)
        full = spread_ref[i].astype(F32) + jnp.dot(hot, merged, preferred_element_type=F32)
        grad[i] = full.astype(BF)
        leave(i).start()
        return carry

    lax.fori_loop(0, half, scatter, 0)

    def drain(i, carry):
        leave(i).wait()
        return carry

    lax.fori_loop(0, half, drain, 0)
    for c in moves:
        c.wait()


def local(
    n_wide,
    n_narrow,
    features,
    adjacency,
    block_rows,
    block_cols,
    block_count,
    node_count,
    halo_index,
    weight,
    bias,
    out_grad,
):
    nodes, width = features.shape
    slots, side, _ = adjacency.shape
    row_blocks = nodes // side
    sides, halo = halo_index.shape[1:]
    halo_blocks = sides * halo // side
    col_blocks = row_blocks + halo_blocks
    vm = pl.BlockSpec(memory_space=pltpu.VMEM)
    sm = pl.BlockSpec(memory_space=pltpu.SMEM)
    hb = pl.BlockSpec(memory_space=ANY)
    dma = pltpu.SemaphoreType.DMA
    shape = jax.ShapeDtypeStruct
    blocked = (row_blocks, side, width)
    lanes = -(-slots // 128) * 128
    slab = width // n_wide
    parts = 2
    across = width // parts
    lines = slab // n_narrow
    scale = 1.0 / math.sqrt(nodes * n_wide * n_narrow)
    step = 4
    chunk = 2 * side
    chunked = (nodes // chunk, chunk, width)
    half = nodes // chunk // 2
    out, own_spread, incoming, gathered, bout = pl.pallas_call(
        functools.partial(layer_kernel, n_wide, n_narrow, scale, step),
        name="layer",
        out_shape=(
            pltpu.VMEM(blocked, BF),
            pltpu.VMEM(blocked, BF),
            pltpu.VMEM((sides, halo, width), BF),
            pltpu.VMEM((parts, n_wide, n_narrow, lines, across), BF),
            pltpu.VMEM((1, width), F32),
        ),
        in_specs=[vm, vm, vm, sm, sm, vm, hb, hb, hb, hb],
        out_specs=(vm,) * 5,
        scratch_shapes=[
            pltpu.VMEM((8, lanes), jnp.int32),
            pltpu.VMEM((8, lanes), jnp.int32),
            pltpu.SMEM((8, lanes), jnp.int32),
            pltpu.VMEM((col_blocks, side, width), BF),
            pltpu.VMEM((slots, side, side), BF),
            pltpu.VMEM((width, width), BF),
            pltpu.VMEM((slots, side, width), F32),
            pltpu.VMEM((sides, halo, width), BF),
            pltpu.VMEM((sides, halo, width), BF),
            pltpu.VMEM((sides, halo, width), BF),
            pltpu.VMEM((parts, width, across), F32),
            pltpu.VMEM((parts, n_wide, slab, across), BF),
            pltpu.VMEM((8, width), F32),
            pltpu.VMEM((1, width), F32),
            pltpu.VMEM((parts, n_wide, slab, across), BF),
            pltpu.VMEM((parts, n_narrow, lines, across), BF),
            pltpu.VMEM((parts, n_narrow, lines, across), BF),
            pltpu.VMEM((parts, n_narrow, lines, across), BF),
            pltpu.VMEM((n_wide, 1, width), F32),
            pltpu.VMEM((1, width), F32),
            pltpu.VMEM((n_narrow, 1, width), F32),
            dma((6,)),
        ]
        + [dma((sides,))] * 2
        + [dma((sides, halo // side))] * 2
        + [dma((parts, n_wide))] * 2
        + [dma((parts, n_narrow))] * 4
        + [dma((parts, n_wide))] * 2
        + [dma((n_wide,))] * 2
        + [dma((n_narrow,))] * 2,
        compiler_params=pltpu.CompilerParams(
            collective_id=0, has_side_effects=True, vmem_limit_bytes=VMEM_LIMIT
        ),
    )(
        halo_index,
        block_rows,
        block_cols,
        block_count,
        node_count,
        bias.reshape(1, width),
        features.reshape(blocked),
        adjacency,
        out_grad.reshape(blocked),
        weight,
    )
    input_grad, out, wout, bout = pl.pallas_call(
        finish_kernel,
        name="finish",
        out_shape=(
            shape(chunked, BF),
            shape(blocked, BF),
            shape((width, width), F32),
            shape((1, width), F32),
        ),
        in_specs=[vm] * 6,
        out_specs=(hb, hb, hb, hb),
        scratch_shapes=[
            pltpu.VMEM((half, chunk, width), BF),
            pltpu.VMEM((width, width), F32),
            dma((4,)),
            dma((half,)),
        ],
        compiler_params=pltpu.CompilerParams(vmem_limit_bytes=FINISH_LIMIT),
    )(halo_index, own_spread.reshape(chunked), incoming, out, gathered, bout)
    return out.reshape(nodes, width), input_grad.reshape(nodes, width), wout, bout.reshape(width)


def solution(mesh):
    both = ("wide", "narrow")
    placed = (
        P(both, None),
        P(both, None, None),
        P(both, None),
        P(both, None),
        P(both),
        P(both),
        P(both, None, None),
        P(),
        P(),
        P(both, None),
    )
    return jax.shard_map(
        functools.partial(local, mesh.shape["wide"], mesh.shape["narrow"]),
        mesh=mesh,
        in_specs=placed,
        out_specs=(P(both, None), P(both, None), P(), P()),
        check_vma=False,
    )
```

```python
import functools
import math

import jax
import jax.numpy as jnp
from jax import lax
from jax.experimental import pallas as pl
from jax.experimental.pallas import tpu as pltpu
from jax.sharding import PartitionSpec as P

MESH = pl.DeviceIdType.MESH
ANY = pl.ANY
VMEM_LIMIT = 48 * 1024 * 1024
FINISH_LIMIT = 16 * 1024 * 1024
BF = jnp.bfloat16
F32 = jnp.float32


def neighbours(n_wide, n_narrow):
    w = lax.axis_index("wide")
    n = lax.axis_index("narrow")
    return (
        (w > 0, (w - 1, n)),
        (w < n_wide - 1, (w + 1, n)),
        (n > 0, (w, n - 1)),
        (n < n_narrow - 1, (w, n + 1)),
    )


def halo_copy(src, dst, send, recv, k, h, target):
    columns = src.shape[2] // 2
    at = pl.ds(h * columns, columns)
    return pltpu.make_async_remote_copy(
        src_ref=src.at[k, :, at],
        dst_ref=dst.at[k ^ 1, :, at],
        send_sem=send.at[k, h],
        recv_sem=recv.at[k ^ 1, h],
        device_id=target,
        device_id_type=MESH,
    )


def tables(row_ref, col_ref, pads, count, row_blocks, col_blocks):
    lanes = pads.shape[1]
    slots = row_ref.shape[1]
    halo_blocks = col_blocks - row_blocks
    pads[...] = jnp.zeros(pads.shape, pads.dtype)
    pads[0:1, 0:slots] = row_ref[...]
    pads[1:2, 0:slots] = col_ref[...]
    lane = lax.broadcasted_iota(jnp.int32, (lanes, lanes), 1)
    sub = lax.broadcasted_iota(jnp.int32, (lanes, lanes), 0)
    one = lambda m: jnp.where(m, 1, 0)
    spread = lambda x: jnp.broadcast_to(x, (lanes, lanes))
    down = lambda x: jnp.sum(x, 0, keepdims=True)
    across = lambda x: jnp.sum(x, 1, keepdims=True)

    row, col = spread(pads[0:1, :]), spread(pads[1:2, :])
    row_t, col_t = jnp.transpose(row), jnp.transpose(col)
    live = lane < count
    own = live & (col < row_blocks)
    own_t = (sub < count) & (col_t < row_blocks)
    before = own_t & (sub < lane)

    def first(a, a_t):
        return own & (spread(down(one(before & (a_t == a)))) == 0)

    def order(key):
        key_t = jnp.transpose(key)
        same = (key == key_t) & (lane < sub)
        rank = across(one((key < key_t) | same))
        twin = jnp.minimum(across(one(same)), 1)
        hot = one(jnp.broadcast_to(rank, (lanes, lanes)) == lane)
        return key_t, rank, twin, lambda x: down(hot * x)

    dead = 2 * col_blocks
    lead = first(row, row_t)
    key_t, rank, twin, pick = order(
        jnp.where(lead, row, jnp.where(live, row + row_blocks, dead))
    )
    at = lane + row_blocks
    has = down(one(key_t == at))
    last = jnp.where(has > 0, down(one(key_t <= at)) - 1, lane[0:1, :])
    prev = jnp.where(twin > 0, rank - 1, row_t)
    lines = [pick(sub), pick(col_t), pick(prev), last]

    lead = first(col, col_t)
    own_key = jnp.where(lead, col + (col_blocks + 1), col + halo_blocks)
    key = jnp.where(col < row_blocks, own_key, col - row_blocks)
    unused = jnp.where(lane < slots, col_blocks, dead)
    key_t, rank, twin, pick = order(jnp.where(live, key, unused))
    has = down(one(key_t == lane))
    ends = jnp.where(has > 0, down(one(key_t <= lane)), 0)
    keep = pick(jnp.broadcast_to(twin, (lanes, lanes)))
    lines += [pick(sub), pick(row_t), keep, ends]
    slot, block = slots - 1, row_blocks - 1
    tops = (slot, col_blocks - 1, slot, slot, slot, block, 1, slots - row_blocks)
    return [jnp.clip(line, 0, top) for line, top in zip(lines, tops)]


def layer_kernel(
    n_wide,
    n_narrow,
    scale,
    step,
    idx_ref,
    row_ref,
    col_ref,
    live,
    nodes_live,
    b_ref,
    feat_hbm,
    adj_hbm,
    grad_hbm,
    w_hbm,
    grad,
    own_spread,
    incoming,
    ag_wide,
    bout_ref,
    pads,
    lined,
    table,
    ext,
    adj,
    w_ref,
    run,
    packed,
    landing,
    ret,
    wsum,
    wg,
    bsum,
    bg,
    rs_wide,
    rs_narrow,
    part,
    ag_narrow,
    b_wide,
    b_mid,
    b_narrow,
    load,
    send,
    recv,
    send_r,
    recv_r,
    send_w,
    recv_w,
    send_n,
    recv_n,
    send_gn,
    recv_gn,
    send_gw,
    recv_gw,
    send_bw,
    recv_bw,
    send_bn,
    recv_bn,
):
    w = lax.axis_index("wide")
    n = lax.axis_index("narrow")
    slots = adj.shape[0]
    row_blocks, side, width = feat_hbm.shape
    col_blocks = ext.shape[0]
    halo_blocks = col_blocks - row_blocks
    half = row_blocks // 2
    count = idx_ref.shape[2]
    per = count // side
    slab, across = rs_wide.shape[2:]
    lines = rs_narrow.shape[2]
    keep_to = nodes_live[0]

    loads = [
        pltpu.make_async_copy(feat_hbm.at[pl.ds(0, half)], ext.at[pl.ds(0, half)], load.at[0]),
        pltpu.make_async_copy(feat_hbm.at[pl.ds(half, half)], ext.at[pl.ds(half, half)], load.at[1]),
        pltpu.make_async_copy(adj_hbm, adj, load.at[2]),
        pltpu.make_async_copy(w_hbm, w_ref, load.at[3]),
        pltpu.make_async_copy(grad_hbm, grad, load.at[4]),
    ]
    loads[0].start()

    def wide_peer(d):
        return (lax.rem(w + d, n_wide), n)

    def narrow_peer(d):
        return (w, lax.rem(n + d, n_narrow))

    def remote(src, dst, s, r, peer):
        return pltpu.make_async_remote_copy(
            src_ref=src, dst_ref=dst, send_sem=s, recv_sem=r, device_id=peer, device_id_type=MESH
        )

    near = neighbours(n_wide, n_narrow)
    peers = [wide_peer(d) for d in range(1, n_wide)] + [
        narrow_peer(d) for d in range(1, n_narrow)
    ]
    barrier = pltpu.get_barrier_semaphore()
    for peer in peers:
        pl.semaphore_signal(barrier, inc=1, device_id=peer, device_id_type=MESH)

    for i, line in enumerate(tables(row_ref, col_ref, pads, live[0], row_blocks, col_blocks)):
        lined[pl.ds(i, 1), :] = line
    tabled = pltpu.make_async_copy(lined, table, load.at[5])
    tabled.start()

    ext[pl.ds(row_blocks, halo_blocks)] = jnp.zeros((halo_blocks, side, width), BF)
    wsum[...] = jnp.zeros_like(wsum)
    bsum[...] = jnp.zeros_like(bsum)
    loads[0].wait()
    for fetch in loads[1:3]:
        fetch.start()
    span = half * side
    lane = lax.broadcasted_iota(jnp.int32, (count, 128), 1).astype(F32)

    def pack(k):
        row = idx_ref[0, pl.ds(k, 1), :].astype(F32)
        column = jnp.transpose(jnp.broadcast_to(row, (128, count)))
        hot = jnp.concatenate(
            [jnp.where(column == lane + float(at), 1.0, 0.0).astype(BF) for at in range(0, span, 128)],
            axis=1,
        )
        near_rows = ext[pl.ds(0, half)].reshape(span, width)
        packed[k] = jnp.dot(hot, near_rows, preferred_element_type=F32).astype(BF)

    pack(2)
    pl.semaphore_wait(barrier, len(peers))
    for k in (2, 3, 1, 0):
        there, target = near[k]
        if k != 2:
            pack(k)

        @pl.when(there)
        def _():
            for h in range(2):
                halo_copy(packed, landing, send, recv, k, h, target).start()

    for fetch in loads[3:]:
        fetch.start()

    def kept(block, blocks=1):
        at = lax.broadcasted_iota(jnp.int32, (blocks * side, width), 0)
        return at < keep_to - block * side

    loads[1].wait()

    def mask(i, carry):
        ext[i] = jnp.where(kept(i), ext[i].astype(F32), 0.0).astype(BF)
        return carry

    lax.fori_loop(half, row_blocks, mask, 0)
    loads[2].wait()
    tabled.wait()

    def product(k):
        return jnp.dot(adj[table[0, k]], ext[table[1, k]], preferred_element_type=F32)

    unroll = 16

    def leading(t, carry):
        for u in range(unroll):
            k = t * unroll + u
            run[k] = product(k)
        return carry

    lax.fori_loop(0, row_blocks // unroll, leading, 0)
    def following(h):
        columns = width // 2
        at = slice(h * columns, (h + 1) * columns)
        for k in (1, 0, 2, 3):
            there, target = near[k]

            @pl.when(there)
            def _():
                halo_copy(packed, landing, send, recv, k, h, target).wait_send()
                halo_copy(packed, landing, send, recv, k ^ 1, h, target).wait_recv()
                ext[pl.ds(row_blocks + k * per, per), :, at] = landing[k, :, at].reshape(
                    per, side, columns
                )

        def body(t, carry):
            for u in range(unroll):
                k = t * unroll + u
                run[k, :, at] = run[table[2, k], :, at] + jnp.dot(
                    adj[table[0, k]], ext[table[1, k], :, at], preferred_element_type=F32
                )
            return carry

        lax.fori_loop(row_blocks // unroll, slots // unroll, body, 0)

    following(0)
    following(1)
    loads[3].wait()
    loads[4].wait()

    tall = step * side

    def into(i, h):
        at = pl.ds(i * step, step)
        if h == 0:
            agg = jnp.concatenate([run[table[3, i * step + j]] for j in range(step)], 0).astype(BF)
            own_spread[at] = agg.reshape(step, side, width)
        else:
            agg = own_spread[at].reshape(tall, width)
        return agg, jnp.dot(agg, w_ref[:, cut(h)], preferred_element_type=F32)

    def cut(h):
        return slice(h * across, (h + 1) * across)

    def middle(i, pre, h):
        at = pl.ds(i * step, step)
        g = grad[at, :, cut(h)].reshape(tall, across).astype(F32)
        pre = pre + b_ref[:, cut(h)]
        at_row = lax.broadcasted_iota(jnp.int32, (tall, across), 0)
        keep = at_row < keep_to - i * tall
        sig = 0.5 * jnp.tanh(0.5 * pre) + 0.5
        act = pre * sig
        grad[at, :, cut(h)] = jnp.where(keep, act, 0.0).astype(BF).reshape(step, side, across)
        dpre = jnp.where(keep, g * (sig + act * (1.0 - sig)), 0.0).astype(BF)
        bsum[:, cut(h)] += jnp.sum(dpre.astype(F32).reshape(tall // 8, 8, across), 0)
        return dpre

    def after(i, agg, dpre, h):
        wsum[h] += lax.dot_general(
            agg, dpre, (((0,), (0,)), ((), ())), preferred_element_type=F32
        )
        ext[pl.ds(i * step, step), :, cut(h)] = dpre.reshape(step, side, across)

    group = row_blocks // step // 2

    def dense(h):
        def body(t, carry):
            now = into(t * group, h)
            for u in range(group):
                i = t * group + u
                later = into(i + 1, h) if u + 1 < group else None
                dpre = middle(i, now[1], h)
                after(i, now[0], dpre, h)
                now = later
            return carry

        lax.fori_loop(0, row_blocks // step // group, body, 0)

    def scatter_wide(h):
        wg[h] = wsum[h].astype(BF).reshape(n_wide, slab, across)
        copies = []
        for d in range(1, n_wide):
            peer = wide_peer(d)
            c = remote(
                wg.at[h, peer[0]], rs_wide.at[h, d], send_w.at[h, d], recv_w.at[h, d], peer
            )
            c.start()
            copies.append(c)
        return copies

    def scatter_narrow(h, arrived):
        total = wg[h, w].astype(F32)
        for c in arrived:
            c.wait_recv()
        for d in range(1, n_wide):
            total = total + rs_wide[h, d].astype(F32)
        for j in range(n_narrow):
            part[h, j] = total[j * lines : (j + 1) * lines].astype(BF)
        copies = []
        for d in range(1, n_narrow):
            peer = narrow_peer(d)
            c = remote(
                part.at[h, peer[1]], rs_narrow.at[h, d], send_n.at[h, d], recv_n.at[h, d], peer
            )
            c.start()
            copies.append(c)
        return copies

    def share_narrow(h, arrived):
        piece = part[h, n].astype(F32)
        for c in arrived:
            c.wait_recv()
        for d in range(1, n_narrow):
            piece = piece + rs_narrow[h, d].astype(F32)
        ag_narrow[h, n] = (piece * scale).astype(BF)
        copies = []
        for d in range(1, n_narrow):
            mine = ag_narrow.at[h, n]
            c = remote(mine, mine, send_gn.at[h, d], recv_gn.at[h, d], narrow_peer(d))
            c.start()
            copies.append(c)
        return copies

    def share_wide(h, arrived):
        for c in arrived:
            c.wait_recv()
        copies = []
        for d in range(1, n_wide):
            c = remote(
                ag_narrow.at[h], ag_wide.at[h, w], send_gw.at[h, d], recv_gw.at[h, d], wide_peer(d)
            )
            c.start()
            copies.append(c)
        ag_wide[h, w] = ag_narrow[h]
        return copies

    dense(0)
    first = [scatter_wide(0)]
    dense(1)
    first.append(scatter_wide(1))
    bg[...] = jnp.sum(bsum[...], 0, keepdims=True)
    bias_first = []
    for d in range(1, n_wide):
        c = remote(bg, b_wide.at[d], send_bw.at[d], recv_bw.at[d], wide_peer(d))
        c.start()
        bias_first.append(c)
    second = [scatter_narrow(0, first[0])]
    run[0] = jnp.zeros(run.shape[1:], run.dtype)
    deep = 8

    def backed(t, carry):
        at = pl.ds(t * deep, deep)
        ext[at] = (
            lax.dot_general(
                ext[at].reshape(deep * side, width),
                w_ref[...],
                (((1,), (1,)), ((), ())),
                preferred_element_type=F32,
            )
            .astype(BF)
            .reshape(deep, side, width)
        )
        return carry

    lax.fori_loop(0, row_blocks // deep, backed, 0)
    third = [share_narrow(0, second[0])]

    def spreading(k):
        return lax.dot_general(
            adj[table[4, k]], ext[table[5, k]], (((0,), (0,)), ((), ())), preferred_element_type=F32
        )

    def backward(t, carry):
        held = run[t * unroll]
        for u in range(unroll):
            k = t * unroll + u
            held = held * table[6, k].astype(F32) + spreading(k)
            run[k + 1] = held
        return carry

    early = slots - row_blocks
    lax.fori_loop(0, early // unroll, backward, 0)
    fourth = [share_wide(0, third[0])]
    second.append(scatter_narrow(1, first[1]))
    bias = bg[...]
    for c in bias_first:
        c.wait_recv()
    for d in range(1, n_wide):
        bias = bias + b_wide[d]
    b_mid[...] = bias
    bias_second = []
    for d in range(1, n_narrow):
        c = remote(b_mid, b_narrow.at[d], send_bn.at[d], recv_bn.at[d], narrow_peer(d))
        c.start()
        bias_second.append(c)

    def returned(k, j):
        at = pl.ds(j * side, side)
        return pltpu.make_async_remote_copy(
            src_ref=ret.at[k, at],
            dst_ref=incoming.at[k ^ 1, at],
            send_sem=send_r.at[k, j],
            recv_sem=recv_r.at[k ^ 1, j],
            device_id=near[k][1],
            device_id_type=MESH,
        )

    def give_back(k, j):
        ret[k, pl.ds(j * side, side), :] = run[table[7, k * per + j]].astype(BF)

        @pl.when(near[k][0])
        def _():
            returned(k, j).start()

        @pl.when(jnp.logical_not(near[k][0]))
        def _():
            incoming[k, pl.ds(j * side, side), :] = jnp.zeros((side, width), BF)

    early_return = [(k, j) for k in (2, 3) for j in range(per // 2)]
    early_return += [(k, j) for k in (1, 0) for j in range(per)]
    for k, j in early_return:
        give_back(k, j)

    def own(c):
        return run[table[7, halo_blocks + c]] + spreading(early + c)

    def low(t, carry):
        for u in range(unroll):
            c = t * unroll + u
            own_spread[c] = own(c).astype(BF)
        return carry

    lax.fori_loop(0, half // unroll, low, 0)
    third.append(share_narrow(1, second[1]))
    for c in bias_second:
        c.wait_recv()
    for d in range(1, n_narrow):
        bias = bias + b_narrow[d]
    bout_ref[...] = bias * scale
    for k in (2, 3):
        for j in range(per // 2, per):
            give_back(k, j)

    def high(t, carry):
        for u in range(unroll):
            c = t * unroll + u
            own_spread[c] = jnp.where(kept(c), own(c), 0.0).astype(BF)
        return carry

    lax.fori_loop(half // unroll, row_blocks // unroll, high, 0)
    fourth.append(share_wide(1, third[1]))
    for k in range(4):
        there, target = near[k]

        @pl.when(there)
        def _():
            for j in range(per):
                returned(k, j).wait_send()
                returned(k ^ 1, j).wait_recv()

    for copies in fourth:
        for c in copies:
            c.wait_recv()
    for copies in first + second + third + fourth + [bias_first, bias_second]:
        for c in copies:
            c.wait_send()


def finish_kernel(
    idx_ref,
    spread_ref,
    incoming,
    out_ref,
    ag_wide,
    b_ref,
    grad_hbm,
    out_hbm,
    w_hbm,
    b_hbm,
    grad,
    wg,
    give,
    part_give,
):
    half, chunk, width = grad.shape
    parts, n_wide, n_narrow, lines, across = ag_wide.shape
    moves = [
        pltpu.make_async_copy(out_ref, out_hbm, give.at[0]),
        pltpu.make_async_copy(
            spread_ref.at[pl.ds(half, half)], grad_hbm.at[pl.ds(half, half)], give.at[1]
        ),
        pltpu.make_async_copy(b_ref, b_hbm, give.at[2]),
    ]
    for c in moves:
        c.start()
    for h in range(parts):
        for i in range(n_wide):
            for j in range(n_narrow):
                at = pl.ds((i * n_narrow + j) * lines, lines)
                wg[at, h * across : (h + 1) * across] = ag_wide[h, i, j].astype(F32)
    moves.append(pltpu.make_async_copy(wg, w_hbm, give.at[3]))
    moves[3].start()
    merged = incoming[...].reshape(-1, width)
    idx = jnp.concatenate([idx_ref[0, k : k + 1, :] for k in range(incoming.shape[0])], 1)

    def leave(i):
        return pltpu.make_async_copy(grad.at[i], grad_hbm.at[i], part_give.at[i])

    def scatter(i, carry):
        row = lax.broadcasted_iota(jnp.int32, (chunk, idx.shape[1]), 0) + i * chunk
        hot = jnp.where(row == idx, 1.0, 0.0).astype(BF)
        full = spread_ref[i].astype(F32) + jnp.dot(hot, merged, preferred_element_type=F32)
        grad[i] = full.astype(BF)
        leave(i).start()
        return carry

    lax.fori_loop(0, half, scatter, 0)

    def drain(i, carry):
        leave(i).wait()
        return carry

    lax.fori_loop(0, half, drain, 0)
    for c in moves:
        c.wait()


def local(
    n_wide,
    n_narrow,
    features,
    adjacency,
    block_rows,
    block_cols,
    block_count,
    node_count,
    halo_index,
    weight,
    bias,
    out_grad,
):
    nodes, width = features.shape
    slots, side, _ = adjacency.shape
    row_blocks = nodes // side
    sides, halo = halo_index.shape[1:]
    halo_blocks = sides * halo // side
    col_blocks = row_blocks + halo_blocks
    vm = pl.BlockSpec(memory_space=pltpu.VMEM)
    sm = pl.BlockSpec(memory_space=pltpu.SMEM)
    hb = pl.BlockSpec(memory_space=ANY)
    dma = pltpu.SemaphoreType.DMA
    shape = jax.ShapeDtypeStruct
    blocked = (row_blocks, side, width)
    lanes = -(-slots // 128) * 128
    slab = width // n_wide
    parts = 2
    across = width // parts
    lines = slab // n_narrow
    scale = 1.0 / math.sqrt(nodes * n_wide * n_narrow)
    step = 4
    chunk = 2 * side
    chunked = (nodes // chunk, chunk, width)
    half = nodes // chunk // 2
    out, own_spread, incoming, gathered, bout = pl.pallas_call(
        functools.partial(layer_kernel, n_wide, n_narrow, scale, step),
        name="layer",
        out_shape=(
            pltpu.VMEM(blocked, BF),
            pltpu.VMEM(blocked, BF),
            pltpu.VMEM((sides, halo, width), BF),
            pltpu.VMEM((parts, n_wide, n_narrow, lines, across), BF),
            pltpu.VMEM((1, width), F32),
        ),
        in_specs=[vm, vm, vm, sm, sm, vm, hb, hb, hb, hb],
        out_specs=(vm,) * 5,
        scratch_shapes=[
            pltpu.VMEM((8, lanes), jnp.int32),
            pltpu.VMEM((8, lanes), jnp.int32),
            pltpu.SMEM((8, lanes), jnp.int32),
            pltpu.VMEM((col_blocks, side, width), BF),
            pltpu.VMEM((slots, side, side), BF),
            pltpu.VMEM((width, width), BF),
            pltpu.VMEM((slots, side, width), F32),
            pltpu.VMEM((sides, halo, width), BF),
            pltpu.VMEM((sides, halo, width), BF),
            pltpu.VMEM((sides, halo, width), BF),
            pltpu.VMEM((parts, width, across), F32),
            pltpu.VMEM((parts, n_wide, slab, across), BF),
            pltpu.VMEM((8, width), F32),
            pltpu.VMEM((1, width), F32),
            pltpu.VMEM((parts, n_wide, slab, across), BF),
            pltpu.VMEM((parts, n_narrow, lines, across), BF),
            pltpu.VMEM((parts, n_narrow, lines, across), BF),
            pltpu.VMEM((parts, n_narrow, lines, across), BF),
            pltpu.VMEM((n_wide, 1, width), F32),
            pltpu.VMEM((1, width), F32),
            pltpu.VMEM((n_narrow, 1, width), F32),
            dma((6,)),
        ]
        + [dma((sides, 2))] * 2
        + [dma((sides, halo // side))] * 2
        + [dma((parts, n_wide))] * 2
        + [dma((parts, n_narrow))] * 4
        + [dma((parts, n_wide))] * 2
        + [dma((n_wide,))] * 2
        + [dma((n_narrow,))] * 2,
        compiler_params=pltpu.CompilerParams(
            collective_id=0, has_side_effects=True, vmem_limit_bytes=VMEM_LIMIT
        ),
    )(
        halo_index,
        block_rows,
        block_cols,
        block_count,
        node_count,
        bias.reshape(1, width),
        features.reshape(blocked),
        adjacency,
        out_grad.reshape(blocked),
        weight,
    )
    input_grad, out, wout, bout = pl.pallas_call(
        finish_kernel,
        name="finish",
        out_shape=(
            shape(chunked, BF),
            shape(blocked, BF),
            shape((width, width), F32),
            shape((1, width), F32),
        ),
        in_specs=[vm] * 6,
        out_specs=(hb, hb, hb, hb),
        scratch_shapes=[
            pltpu.VMEM((half, chunk, width), BF),
            pltpu.VMEM((width, width), F32),
            dma((4,)),
            dma((half,)),
        ],
        compiler_params=pltpu.CompilerParams(vmem_limit_bytes=FINISH_LIMIT),
    )(halo_index, own_spread.reshape(chunked), incoming, out, gathered, bout)
    return out.reshape(nodes, width), input_grad.reshape(nodes, width), wout, bout.reshape(width)


def solution(mesh):
    both = ("wide", "narrow")
    placed = (
        P(both, None),
        P(both, None, None),
        P(both, None),
        P(both, None),
        P(both),
        P(both),
        P(both, None, None),
        P(),
        P(),
        P(both, None),
    )
    return jax.shard_map(
        functools.partial(local, mesh.shape["wide"], mesh.shape["narrow"]),
        mesh=mesh,
        in_specs=placed,
        out_specs=(P(both, None), P(both, None), P(), P()),
        check_vma=False,
    )
```
